512 devices in a mesh: gx: 4 (over y_hi), gy: 8 (over z), gz: 16 (over y_lo, x, core).
Axes of the slice: x: 4, y: 8 (y_hi: 4, y_lo: 2; y = y_hi * 2 + y_lo), z: 8, core: 2. Of those that a mesh axis runs over, the one named last changes fastest.
Arguments:
- dual_blocks: bfloat16 [4, 8, 16, 1024, 1024], P('gx', 'gy', 'gz'), may hold values from -1 to 3, as said below
- load_terms: bfloat16 [4, 8, 16, 1024, 128], P('gx', 'gy', 'gz'), may hold values from -6 to 6
- row_order: int32 [4, 8, 16, 1024], P('gx', 'gy', 'gz'), may hold values from 0 to 1023, each once within a row
- mode_rows: bfloat16 [4, 8, 16, 1024, 6], P('gx', 'gy', 'gz'), may hold values from -0.1875 to 0.1875
- mode_count: int32 [4, 8, 16], P('gx', 'gy', 'gz'), may hold values from 0 to 6, as said below
- coarse_inverse: float32 [4, 8, 96, 96], P('gx', 'gy'), may hold values from -1 to 3, as said below
Outputs:
- multipliers: float32 [4, 8, 16, 1024, 128], P('gx', 'gy', 'gz')
- residual: float32 [4, 8, 16, 1024, 128], P('gx', 'gy', 'gz')
The draws below stay inside these ranges and needn't reach their ends.
Inputs may be any that keep to these rules, and one draw needn't show every extreme that they name: `mode_count`: subdomains away from the outer boundary have 6 rigid-body modes; subdomains on the outer boundary have 0 to 6; some subdomain has exactly 6 and some boundary subdomain has none. Each subdomain's row of row_order is a permutation of its 1024 rows. `dual_blocks`: each subdomain's block is symmetric positive definite. `coarse_inverse`: each line's matrix is symmetric positive definite.
All inputs are finite; a program needn't handle non-finite values.
Results may differ from the reference program's by a relative error of at most 0.0082.
Values sent between devices are 32-bit elements; how exact they have to be, the bound alone decides.
No kernel may reach another device: no remote copies, remote signals or barrier semaphores. Data moves between devices by JAX's collectives and lax.ppermute only.
A program may use at most 64 MiB of HBM per device.

```python
import math
import jax
import jax.numpy as jnp
from jax import lax

FACE = 128
EDGE = 16
CORNER = 8
M = 1024
LOADS = 128
NMODE = 6
ITERS = 3
SUB_X = 4
SUB_Y = 8
SUB_Z = 16
COARSE = 96


def draw_dual_blocks(key, part):
    sub_total = SUB_X * SUB_Y * SUB_Z

    def draw_one(index_value):
        sub_key = jax.random.fold_in(key, index_value)
        key_noise, key_diag = jax.random.split(sub_key)
        noise_part = jax.random.normal(key_noise, (M, M), jnp.float32)
        diag_vals = jax.random.uniform(key_diag, (M,), jnp.float32, 1.0, 2.0)
        noise_part = noise_part * (0.3 / math.sqrt(M))
        symmetric = (noise_part + noise_part.T) * 0.70710678
        identity = jnp.eye(M, dtype=jnp.float32)
        return (symmetric + identity * diag_vals[None, :]).astype(jnp.bfloat16)
    blocks = lax.map(draw_one, jnp.arange(sub_total, dtype=jnp.int32))
    return blocks.reshape(SUB_X, SUB_Y, SUB_Z, M, M)


def draw_mode_count(key, part):
    keys = jax.random.split(jax.random.fold_in(key, 17), 7)
    pos_x = jnp.arange(SUB_X, dtype=jnp.int32)[:, None, None]
    pos_y = jnp.arange(SUB_Y, dtype=jnp.int32)[None, :, None]
    pos_z = jnp.arange(SUB_Z, dtype=jnp.int32)[None, None, :]
    boundary = (pos_x == 0) | (pos_x == SUB_X - 1) | (pos_y == 0) | (pos_y == SUB_Y - 1) | (pos_z == 0) | (pos_z == SUB_Z - 1)
    coin = jax.random.randint(keys[0], (SUB_X, SUB_Y, SUB_Z), 0, 2)
    fewer = jax.random.randint(keys[1], (SUB_X, SUB_Y, SUB_Z), 0, NMODE)
    counts = jnp.where(boundary & (coin == 1), fewer, NMODE)
    high_x = jax.random.randint(keys[2], (), 0, SUB_X)
    high_y = jax.random.randint(keys[3], (), 0, SUB_Y)
    high_z = jax.random.randint(keys[4], (), 0, SUB_Z)
    low_x = jax.random.randint(keys[5], (), 0, SUB_X)
    low_y = jax.random.randint(keys[6], (), 0, SUB_Y)
    low_z = jnp.where(high_z == 0, SUB_Z - 1, 0)
    counts = jnp.where((pos_x == high_x) & (pos_y == high_y) & (pos_z == high_z), NMODE, counts)
    counts = jnp.where((pos_x == low_x) & (pos_y == low_y) & (pos_z == low_z), 0, counts)
    return counts.astype(jnp.int32)


def draw_coarse_inverse(key, part):
    key_base, key_diag = jax.random.split(jax.random.fold_in(key, 29))
    base_draw = jax.random.normal(key_base, (SUB_X, SUB_Y, COARSE, COARSE), jnp.float32)
    diag_vals = jax.random.uniform(key_diag, (SUB_X, SUB_Y, COARSE), jnp.float32, 0.05, 0.15)
    wishart = jnp.einsum('abij,abkj->abik', base_draw, base_draw) * (0.4 / COARSE)
    identity = jnp.eye(COARSE, dtype=jnp.float32)
    return wishart + identity[None, None] * diag_vals[..., None, :]


def shard_levels(stream_key, dims, pieces, low, largest):
    gain, own = 1.0, jax.random.fold_in(stream_key, 6)
    for dim, parts in pieces:
        draws = jnp.exp(jax.random.uniform(jax.random.fold_in(own, dim), (parts,), jnp.float32, low / len(pieces), largest / len(pieces)))
        gain = gain * jnp.repeat(draws, dims[dim] // parts).reshape([-1 if axis == dim else 1 for axis in range(len(dims))])
    return gain


def noise(key, shape, scale, most, cuts=(), kind=jnp.bfloat16):
    result = jax.random.normal(key, shape, jnp.float32) * scale
    if len(cuts) > 0:
        result = shard_levels(key, shape, cuts, -0.22, 0.18) * result
    return jnp.clip(result, min=-most, max=most).astype(kind)


def setup_inputs(seed: int = 0) -> dict:
    seeds = jax.random.split(jax.random.key(seed), 7)
    return {
        "dual_blocks": draw_dual_blocks(jax.random.fold_in(seeds[6], 71), 0),
        "load_terms": noise(seeds[1], (SUB_X, SUB_Y, SUB_Z, M, LOADS), 1.0, 6.0, ((0, 4), (1, 8), (2, 16))),
        "row_order": jax.vmap(lambda own: jax.random.permutation(own, M))(jax.random.split(seeds[2], SUB_X * SUB_Y * SUB_Z)).reshape((SUB_X, SUB_Y, SUB_Z, M)).astype(jnp.int32),
        "mode_rows": noise(seeds[3], (SUB_X, SUB_Y, SUB_Z, M, NMODE), M ** -0.5, 0.1875, ((0, 4), (1, 8), (2, 16))),
        "mode_count": draw_mode_count(jax.random.fold_in(seeds[6], 71), 0),
        "coarse_inverse": draw_coarse_inverse(jax.random.fold_in(seeds[6], 71), 0),
    }


EIG_LOW = 0.5
EIG_HIGH = 6.0


def slot_table():
    slot_list = []
    begin_row = 0
    for weight_class, width_rows in ((1, FACE), (2, EDGE), (3, CORNER)):
        for sign_one in (-1, 0, 1):
            for sign_two in (-1, 0, 1):
                for sign_three in (-1, 0, 1):
                    if abs(sign_one) + abs(sign_two) + abs(sign_three) == weight_class:
                        slot_list.append(((sign_one, sign_two, sign_three), begin_row, width_rows))
                        begin_row += width_rows
    return slot_list


def partner_rows(packed):
    padded = jnp.pad(packed, ((1, 1), (1, 1), (1, 1), (0, 0), (0, 0)))
    slot_list = slot_table()
    lookup = {}
    for offset, begin_row, width_rows in slot_list:
        lookup[offset] = begin_row
    blocks = []
    for offset, begin_row, width_rows in slot_list:
        other_begin = lookup[(-offset[0], -offset[1], -offset[2])]
        segment = padded[1 + offset[0]:1 + offset[0] + SUB_X, 1 + offset[1]:1 + offset[1] + SUB_Y,
                         1 + offset[2]:1 + offset[2] + SUB_Z, other_begin:other_begin + width_rows]
        blocks.append(segment)
    return jnp.concatenate(blocks, axis=3)


def pack_rows(values, row_order):
    return jnp.take_along_axis(values, row_order[..., None], axis=3)


def apply_operator(dual_blocks, row_order, direction):
    sub_total = SUB_X * SUB_Y * SUB_Z
    flat_dual = dual_blocks.reshape(sub_total, M, M)
    flat_order = row_order.reshape(sub_total, M)
    rounded = lax.optimization_barrier(direction.astype(jnp.bfloat16))
    flat_vectors = rounded.reshape(sub_total, M, direction.shape[-1])

    def multiply(operands):
        dual_one, packing, vector = operands
        packed_block = jnp.take(jnp.take(dual_one, packing, axis=0), packing, axis=1).astype(jnp.float32)
        return jnp.dot(packed_block, vector.astype(jnp.float32), precision=lax.Precision.HIGHEST)

    images = lax.map(multiply, (flat_dual, flat_order, flat_vectors)).reshape(direction.shape)
    return images + partner_rows(images)


def coarse_step(residual, mode_cols, mode_count, coarse_inverse):
    highest = lax.Precision.HIGHEST
    project = jnp.einsum("abcmk,abcmr->abckr", mode_cols, residual, precision=highest)
    offsets = jnp.cumsum(mode_count, axis=2) - mode_count
    compact_pos = jnp.arange(COARSE, dtype=jnp.int32)
    mode_index = jnp.arange(NMODE, dtype=jnp.int32)
    hits = compact_pos[None, None, None, None, :] == offsets[..., None, None] + mode_index[None, None, None, :, None]
    valid = mode_index[None, None, None, :, None] < mode_count[..., None, None]
    select = jnp.where(hits & valid, 1.0, 0.0).astype(jnp.float32)
    compact = jnp.einsum("abckj,abckr->abjr", select, project, precision=highest)
    solved = jnp.einsum("abij,abjr->abir", coarse_inverse, compact, precision=highest)
    amplitude = jnp.einsum("abckj,abjr->abckr", select, solved, precision=highest)
    spread = jnp.einsum("abcmk,abckr->abcmr", mode_cols, amplitude, precision=highest)
    return residual - spread - partner_rows(spread)


def reference(dual_blocks, load_terms, row_order, mode_rows, mode_count, coarse_inverse):
    load_rows = pack_rows(load_terms.astype(jnp.float32), row_order)
    mode_cols = pack_rows(mode_rows.astype(jnp.float32), row_order)
    center_value = 0.5 * (EIG_HIGH + EIG_LOW)
    half_width = 0.5 * (EIG_HIGH - EIG_LOW)
    residual = load_rows + partner_rows(load_rows)
    direction = coarse_step(residual, mode_cols, mode_count, coarse_inverse) / center_value
    multipliers = direction
    rho_prev = half_width / center_value
    residual = residual - apply_operator(dual_blocks, row_order, direction)
    for iteration in range(1, ITERS):
        corrected = coarse_step(residual, mode_cols, mode_count, coarse_inverse)
        rho_now = 1.0 / (2.0 * center_value / half_width - rho_prev)
        direction = (rho_now * rho_prev) * direction + (2.0 * rho_now / half_width) * corrected
        multipliers = multipliers + direction
        residual = residual - apply_operator(dual_blocks, row_order, direction)
        rho_prev = rho_now
    unpacking = jnp.argsort(row_order, axis=-1).astype(jnp.int32)
    return (jnp.take_along_axis(multipliers, unpacking[..., None], axis=3),
            jnp.take_along_axis(residual, unpacking[..., None], axis=3))
```

```python
import functools

import jax
import jax.numpy as jnp
import numpy as np
from jax import lax
from jax.experimental import pallas as pl
from jax.experimental.pallas import tpu as pltpu
from jax.sharding import PartitionSpec as P

FACE = 128
EDGE = 16
CORNER = 8
NMODE = 6
ITERS = 3
EIG_LOW = 0.5
EIG_HIGH = 6.0

F32 = jnp.float32
BF16 = jnp.bfloat16
HIGHEST = lax.Precision.HIGHEST
SIGNS = (1, -1, 0)
WIDTHS = {1: FACE, 2: EDGE, 3: CORNER}

BUNDLE = 224
GROUP = 8


def tables():
    begin, row = {}, 0
    for weight in (1, 2, 3):
        for o1 in (-1, 0, 1):
            for o2 in (-1, 0, 1):
                for o3 in (-1, 0, 1):
                    if abs(o1) + abs(o2) + abs(o3) == weight:
                        begin[(o1, o2, o3)] = row
                        row += WIDTHS[weight]
    slots, ours, row = [], {}, 0
    for o1 in SIGNS:
        for o2 in SIGNS:
            for o3 in SIGNS:
                offset = (o1, o2, o3)
                if any(offset):
                    width = WIDTHS[abs(o1) + abs(o2) + abs(o3)]
                    slots.append((offset, begin[offset], width))
                    ours[offset] = row
                    row += width
    return slots, ours, row


SLOTS, OURS, ROWS = tables()


def swaps(size, parity):
    pairs = [(i, i + 1) for i in range(parity, size - 1, 2)]
    return pairs + [(j, i) for i, j in pairs]


def exchange(first, second, axis):
    size = lax.axis_size(axis)
    return lax.ppermute(first, axis, swaps(size, 0)), lax.ppermute(second, axis, swaps(size, 1))


VMEM = pl.BlockSpec(memory_space=pltpu.VMEM)
SMEM = pl.BlockSpec(memory_space=pltpu.SMEM)


def call(kernel, out_shape, scalars, *args, scratch=(), name=None, limit=24):
    return pl.pallas_call(
        kernel,
        out_shape=[jax.ShapeDtypeStruct(s, t) for s, t in out_shape],
        in_specs=[SMEM] + [VMEM] * len(args),
        out_specs=[VMEM] * len(out_shape),
        scratch_shapes=list(scratch),
        compiler_params=pltpu.CompilerParams(vmem_limit_bytes=limit * 2**20),
        name=name,
    )(scalars, *args)


def split3(x):
    high = x.astype(BF16)
    rest = x - high.astype(F32)
    mid = rest.astype(BF16)
    return high, mid, (rest - mid.astype(F32)).astype(BF16)


def dot(a, b):
    return jnp.dot(a, b, preferred_element_type=F32)


def dot_t(a, b):
    return lax.dot_general(a, b, (((1,), (1,)), ((), ())), preferred_element_type=F32)


def dot_exact(a, x):
    high, mid, low = split3(x)
    return dot(a, high) + dot(a, mid) + dot(a, low)


def iota(shape, dim):
    return lax.broadcasted_iota(jnp.int32, shape, dim)


def layers(extra):
    return [(1, 0), (GROUP, BUNDLE)] if extra else [(1, 0)]


def bundle_rows(extra):
    return BUNDLE + BUNDLE // GROUP if extra else BUNDLE


def put(ref, at, pieces):
    for piece in pieces:
        ref[at : at + piece.shape[0], :] = piece
        at += piece.shape[0]


def put_pair(ref_a, ref_b, at, parity, plus, minus):
    even = parity == 0
    put(ref_a, at, [jnp.where(even, p, m) for p, m in zip(plus, minus)])
    put(ref_b, at, [jnp.where(even, m, p) for p, m in zip(plus, minus)])


def received(ref_a, ref_b, parity, scale, base):
    even = parity == 0

    def cut(ref, a, b):
        return ref[base + a // scale : base + b // scale, :]

    def up(a, b):
        return jnp.where(even, cut(ref_b, a, b), cut(ref_a, a, b))

    def down(a, b):
        return jnp.where(even, cut(ref_a, a, b), cut(ref_b, a, b))

    return up, down


def send_x(parity, values, send_a, send_b, extra):
    for value, (scale, base) in zip(values, layers(extra)):
        width = BUNDLE // scale
        put_pair(send_a, send_b, base, parity, [value[0:width, :]], [value[width : 2 * width, :]])


def route_y(extra, sc, *refs):
    count = 2 if extra else 1
    values, (xa, xb, ya, yb) = refs[:count], refs[count:]
    for value, (scale, base) in zip(values, layers(extra)):
        up, down = received(xa, xb, sc[0], scale, base)
        plus = [up(0, 32), down(0, 32), value[448 // scale : 608 // scale, :]]
        minus = [up(32, 64), down(32, 64), value[608 // scale : 768 // scale, :]]
        put_pair(ya, yb, base, sc[1], plus, minus)


def route_z(extra, sc, *refs):
    count = 2 if extra else 1
    values, (xa, xb, ya, yb, za, zb) = refs[:count], refs[count:]
    for value, (scale, base) in zip(values, layers(extra)):
        x_up, x_down = received(xa, xb, sc[0], scale, base)
        y_up, y_down = received(ya, yb, sc[1], scale, base)
        both = []
        for x_at, y_at, own in ((64, (0, 32, 64), 768), (80, (8, 40, 80), 896)):
            pieces = [x_up(x_at, x_at + EDGE), x_down(x_at, x_at + EDGE)]
            for y in (y_up, y_down):
                for at, width in zip(y_at, (CORNER, CORNER, EDGE)):
                    pieces.append(y(at, at + width))
            pieces.append(value[own // scale : (own + FACE) // scale, :])
            both.append(pieces)
        put_pair(za, zb, base, sc[2], both[0], both[1])


def partner_pieces(sc, xa, xb, ya, yb, za, zb, scale, base):
    x_up, x_down = received(xa, xb, sc[0], scale, base)
    y_up, y_down = received(ya, yb, sc[1], scale, base)
    z_up, z_down = received(za, zb, sc[2], scale, base)
    pieces = []
    for (o1, o2, o3), _, width in SLOTS:
        s1, s2, s3 = -o1, -o2, -o3
        if s3:
            reader = z_up if s3 == 1 else z_down
            if s2:
                at = 32 if s2 == 1 else 64
                at += {1: 0, -1: CORNER, 0: 2 * CORNER}[s1]
            elif s1:
                at = 0 if s1 == 1 else EDGE
            else:
                at = 96
        elif s2:
            reader = y_up if s2 == 1 else y_down
            at = {1: EDGE, -1: 32 + EDGE, 0: 96}[s1]
        else:
            reader = x_up if s1 == 1 else x_down
            at = 96
        pieces.append(reader(at, at + width))
    return pieces


def pack_kernel(sc, order_col, order_row, load, modes, sel_ref, inv_ref, load_ref, comp_ref, bt_ref, b_ref, xa, xb):
    step = 256
    for at in range(0, ROWS, step):
        lanes = iota((step, ROWS), 1)
        sel_ref[at : at + step, :] = jnp.where(order_col[at : at + step, :] == lanes, 1.0, 0.0).astype(BF16)
        subs = iota((step, ROWS), 0) + at
        inv_ref[at : at + step, :] = jnp.where(order_row[...] == subs, 1.0, 0.0).astype(BF16)
    sel = sel_ref[...]
    load_ref[...] = dot(sel, load[...])
    bt_ref[...] = dot(modes[...], inv_ref[...]).astype(BF16)
    cols = dot_t(sel, modes[...]).astype(BF16)
    b_ref[...] = cols
    spread = jnp.where(iota((16, 128), 0) == iota((16, 128), 1) % 16, 1.0, 0.0).astype(BF16)
    wide = dot(cols, spread)
    keep = iota((ROWS, 128), 0) % GROUP == iota((ROWS, 128), 1) // 16
    wide = jnp.where(keep, wide, 0.0).astype(BF16)
    fold = jnp.where(iota((ROWS // GROUP, ROWS), 0) == iota((ROWS // GROUP, ROWS), 1) // GROUP, 1.0, 0.0)
    comp_ref[...] = dot(fold.astype(BF16), wide)
    send_x(sc[0], (load_ref, comp_ref), xa, xb, True)


def permute_kernel(sc, sel, inv, dual, out):
    step = 256
    for at in range(0, ROWS, step):
        rows = dot(sel[at : at + step, :], dual[...]).astype(BF16)
        out[at : at + step, :] = dot(rows, inv[...]).astype(BF16)


def project(sc, bt, residual, out):
    block = dot_exact(bt[...], residual)[0:8, :]
    count = sc[4].astype(F32)
    block = jnp.where(iota((8, 128), 0) == NMODE, count, block)
    for t in range(out.shape[0]):
        out[t, :, :] = block


def first_kernel(sc, load, bt, xa, xb, ya, yb, za, zb, res_ref, comp_ref, out):
    pieces = partner_pieces(sc, xa, xb, ya, yb, za, zb, 1, 0)
    at = 0
    for piece in pieces:
        end = at + piece.shape[0]
        res_ref[at:end, :] = load[at:end, :] + piece
        at = end
    project(sc, bt, res_ref[...], out)
    put(comp_ref, 0, partner_pieces(sc, xa, xb, ya, yb, za, zb, GROUP, BUNDLE))


def next_residual(sc, res, val, bundles, out):
    at = 0
    for piece in partner_pieces(sc, *bundles, 1, 0):
        end = at + piece.shape[0]
        out[at:end, :] = res[at:end, :] - (val[at:end, :] + piece)
        at = end


def step_kernel(sc, res, val, bt, xa, xb, ya, yb, za, zb, res_ref, out):
    next_residual(sc, res, val, (xa, xb, ya, yb, za, zb), res_ref)
    project(sc, bt, res_ref[...], out)


def last_kernel(sc, res, val, inv, xa, xb, ya, yb, za, zb, out, scratch):
    next_residual(sc, res, val, (xa, xb, ya, yb, za, zb), scratch)
    out[...] = dot_exact(inv[...], scratch[...])


def unpack_kernel(sc, inv, val, out):
    out[...] = dot_exact(inv[...], val[...])


def mode_kernel(sc, cols, comp, block, out):
    pick = jnp.where(iota((ROWS, 128), 0) // GROUP == iota((ROWS, 128), 1), 1.0, 0.0).astype(BF16)
    wide = dot(pick, comp[...].astype(BF16))
    keep = iota((ROWS, 128), 0) % GROUP == iota((ROWS, 128), 1) // 16
    wide = jnp.where(keep, wide, 0.0).astype(BF16)
    mode = iota((128, 256), 0) % 16
    fold = jnp.where((mode == iota((128, 256), 1) % 8) & (mode < NMODE), 1.0, 0.0).astype(BF16)
    theirs = dot(wide, fold)
    mode = iota((16, 256), 0)
    own = jnp.where((mode == iota((16, 256), 1) % 8) & (mode < NMODE), 1.0, 0.0).astype(BF16)
    mine = dot(cols[...], own)
    x_even, y_even = sc[0] == 0, sc[1] == 0
    which = jnp.where(
        x_even,
        jnp.where(y_even, block[:, 0:1], block[:, 1:2]),
        jnp.where(y_even, block[:, 2:3], block[:, 3:4]),
    )
    at = iota((ROWS, 256), 1) // 8
    out[...] = (jnp.where(at == which, theirs, 0.0) + jnp.where(at == 1, mine, 0.0)).astype(BF16)


def line_kernel(sc, line, inverse, mat_ref, out):
    everyone = line[...]
    size, coarse = everyone.shape[0], inverse.shape[0]

    def selection(rows, first):
        row = iota((rows, size), 0) + first
        col = iota((rows, size), 1)
        is_count = col % 8 == NMODE
        here = jnp.where(is_count & (col // 8 == row // 8), 1.0, 0.0)
        before = jnp.where(is_count & (col // 8 < row // 8), 1.0, 0.0)
        count = jnp.dot(here, everyone, precision=HIGHEST, preferred_element_type=F32)
        offset = jnp.dot(before, everyone, precision=HIGHEST, preferred_element_type=F32)
        mode = ((iota((rows, 128), 0) + first) % 8).astype(F32)
        compact = iota((rows, 128), 1).astype(F32)
        hit = (compact == offset + mode) & (mode < count)
        return jnp.where(hit, 1.0, 0.0)[:, 0:coarse]

    everywhere = selection(size, 0)
    near = selection(24, 8 * sc[3] - 8)
    rows = jnp.dot(near, inverse[...], precision=HIGHEST, preferred_element_type=F32)
    matrix = lax.dot_general(rows, everywhere, (((1,), (1,)), ((), ())), precision=HIGHEST, preferred_element_type=F32)
    mat_ref[...] = matrix
    out[...] = jnp.dot(matrix, everyone, precision=HIGHEST, preferred_element_type=F32)


def solve_kernel(sc, line, matrix, out):
    out[...] = jnp.dot(matrix[...], line[...], precision=HIGHEST, preferred_element_type=F32)


def advance_kernel(keep, take, sc, *refs):
    if keep:
        res, modes, dual, own, ya, yb, xa, xb, old_dir, old_mul, dir_ref, mul_ref, val_ref, sa, sb, stack = refs
    else:
        res, modes, dual, own, ya, yb, xa, xb, dir_ref, val_ref, sa, sb, stack = refs
    put(stack, 0, [own[...], ya[...], yb[...], xa[...], xb[...], jnp.zeros((40, 128), F32)])
    corrected = res[...] - dot_exact(modes[...], stack[...])
    if keep:
        direction = keep * old_dir[...] + take * corrected
        mul_ref[...] = old_mul[...] + direction
    else:
        direction = corrected / take
    dir_ref[...] = direction
    val_ref[...] = dot(dual[...], direction.astype(BF16))
    send_x(sc[0], (val_ref,), sa, sb, False)


def cross(sc, values, sent, extra):
    rows = bundle_rows(extra)
    pair = [((rows, 128), F32)] * 2
    x = exchange(*sent, "gx")
    y = exchange(*call(functools.partial(route_y, extra), pair, sc, *values, *x, name="route_y"), "gy")
    z = exchange(*call(functools.partial(route_z, extra), pair, sc, *values, *x, *y, name="route_z"), "gz")
    return (*x, *y, *z)


def amplitude_blocks():
    out = np.zeros((ROWS, 4), np.int32)
    for x_odd in (0, 1):
        for y_odd in (0, 1):
            for (o1, o2, o3), _, width in SLOTS:
                at = OURS[(o1, o2, o3)]
                lab1 = 0 if o1 == 0 else 1 + ((o1 == -1) ^ x_odd)
                lab2 = 0 if o2 == 0 else 1 + ((o2 == -1) ^ y_odd)
                out[at : at + width, 2 * x_odd + y_odd] = 3 * (3 * lab1 + lab2) + o3 + 1
    return out


def local(dual_blocks, load_terms, row_order, mode_rows, mode_count, coarse_inverse):
    line_length = lax.axis_size("gz")
    pos = [lax.axis_index(axis) for axis in ("gx", "gy", "gz")]
    sc = jnp.stack([p % 2 for p in pos] + [pos[2], mode_count[0, 0, 0]]).astype(jnp.int32)
    packing = row_order[0, 0, 0]
    order = jnp.concatenate([packing[begin : begin + width] for _, begin, width in SLOTS])
    modes = jnp.pad(mode_rows[0, 0, 0].T, ((0, 16 - NMODE), (0, 0)))
    inverse = coarse_inverse[0, 0]
    bundle = [((BUNDLE, 128), F32)] * 2
    vector = ((ROWS, 128), F32)
    square = ((ROWS, ROWS), BF16)
    wide = [((bundle_rows(True), 128), F32)] * 2
    gathered = ((line_length, 8, 128), F32)

    sel, inv, load_rows, comp, bt, cols, sa, sb = call(
        pack_kernel,
        [square, square, vector, ((ROWS // GROUP, 128), F32), ((16, ROWS), BF16), ((ROWS, 16), BF16), *wide],
        sc,
        order[:, None],
        order[None, :],
        load_terms[0, 0, 0],
        modes,
        name="pack",
    )
    (dual,) = call(permute_kernel, [square], sc, sel, inv, dual_blocks[0, 0, 0], name="permute")
    received_rows = cross(sc, (load_rows, comp), (sa, sb), True)
    residual, their_comp, proj = call(
        first_kernel,
        [vector, ((ROWS // GROUP, 128), F32), gathered],
        sc,
        load_rows,
        bt,
        *received_rows,
        name="first",
    )
    (modes_near,) = call(
        mode_kernel, [((ROWS, 256), BF16)], sc, cols, their_comp, jnp.asarray(amplitude_blocks()), name="modes"
    )

    center_value = 0.5 * (EIG_HIGH + EIG_LOW)
    half_width = 0.5 * (EIG_HIGH - EIG_LOW)
    rho_prev = half_width / center_value
    amp = ((24, 128), F32)
    for iteration in range(ITERS):
        line = lax.all_to_all(proj, "gz", 0, 0, tiled=True).reshape(8 * line_length, 128)
        if iteration == 0:
            matrix, own = call(line_kernel, [((24, 8 * line_length), F32), amp], sc, line, inverse, name="line")
        else:
            (own,) = call(solve_kernel, [amp], sc, line, matrix, name="solve")
        ya, yb = exchange(own, own, "gy")
        column = jnp.concatenate([own, ya, yb], axis=0)
        xa, xb = exchange(column, column, "gx")
        near = (modes_near, dual, own, ya, yb, xa, xb)
        scratch = [pltpu.VMEM((256, 128), F32)]
        if iteration == 0:
            direction, value, sa, sb = call(
                functools.partial(advance_kernel, None, center_value),
                [vector, vector, *bundle],
                sc,
                residual,
                *near,
                scratch=scratch,
                name="advance0",
            )
            multipliers = direction
        else:
            rho_now = 1.0 / (2.0 * center_value / half_width - rho_prev)
            direction, multipliers, value, sa, sb = call(
                functools.partial(advance_kernel, rho_now * rho_prev, 2.0 * rho_now / half_width),
                [vector, vector, vector, *bundle],
                sc,
                residual,
                *near,
                direction,
                multipliers,
                scratch=scratch,
                name="advance",
            )
            rho_prev = rho_now
        received_rows = cross(sc, (value,), (sa, sb), False)
        if iteration < ITERS - 1:
            residual, proj = call(
                step_kernel, [vector, gathered], sc, residual, value, bt, *received_rows, name="step"
            )
    (out_mul,) = call(unpack_kernel, [vector], sc, inv, multipliers, name="unpack")
    (out_res,) = call(
        last_kernel,
        [vector],
        sc,
        residual,
        value,
        inv,
        *received_rows,
        scratch=[pltpu.VMEM((ROWS, 128), F32)],
        name="last",
    )
    return out_mul[None, None, None], out_res[None, None, None]


def solution(mesh):
    in_specs = (
        P("gx", "gy", "gz", None, None),
        P("gx", "gy", "gz", None, None),
        P("gx", "gy", "gz", None),
        P("gx", "gy", "gz", None, None),
        P("gx", "gy", "gz"),
        P("gx", "gy", None, None),
    )
    out_specs = (P("gx", "gy", "gz", None, None), P("gx", "gy", "gz", None, None))
    return jax.shard_map(local, mesh=mesh, in_specs=in_specs, out_specs=out_specs, check_vma=False)
```

```python
import functools

import jax
import jax.numpy as jnp
import numpy as np
from jax import lax
from jax.experimental import pallas as pl
from jax.experimental.pallas import tpu as pltpu
from jax.sharding import PartitionSpec as P

FACE = 128
EDGE = 16
CORNER = 8
NMODE = 6
ITERS = 3
EIG_LOW = 0.5
EIG_HIGH = 6.0

F32 = jnp.float32
BF16 = jnp.bfloat16
HIGHEST = lax.Precision.HIGHEST
SIGNS = (1, -1, 0)
WIDTHS = {1: FACE, 2: EDGE, 3: CORNER}

BUNDLE = 224
GROUP = 8


def tables():
    begin, row = {}, 0
    for weight in (1, 2, 3):
        for o1 in (-1, 0, 1):
            for o2 in (-1, 0, 1):
                for o3 in (-1, 0, 1):
                    if abs(o1) + abs(o2) + abs(o3) == weight:
                        begin[(o1, o2, o3)] = row
                        row += WIDTHS[weight]
    slots, ours, row = [], {}, 0
    for o1 in SIGNS:
        for o2 in SIGNS:
            for o3 in SIGNS:
                offset = (o1, o2, o3)
                if any(offset):
                    width = WIDTHS[abs(o1) + abs(o2) + abs(o3)]
                    slots.append((offset, begin[offset], width))
                    ours[offset] = row
                    row += width
    return slots, ours, row


SLOTS, OURS, ROWS = tables()


def swaps(size, parity):
    pairs = [(i, i + 1) for i in range(parity, size - 1, 2)]
    return pairs + [(j, i) for i, j in pairs]


def exchange(first, second, axis):
    size = lax.axis_size(axis)
    groups = [[i, i + 1] for i in range(0, size, 2)]
    other = lax.ppermute(second, axis, swaps(size, 1))
    return lax.all_gather(first, axis, axis_index_groups=groups, tiled=True), other


def exchange_async(first, second, axis):
    size = lax.axis_size(axis)
    return lax.ppermute(first, axis, swaps(size, 0)), lax.ppermute(second, axis, swaps(size, 1))


VMEM = pl.BlockSpec(memory_space=pltpu.VMEM)
HBM = pl.BlockSpec(memory_space=pltpu.HBM)
SMEM = pl.BlockSpec(memory_space=pltpu.SMEM)


def call(kernel, out_shape, scalars, *args, scratch=(), name=None, limit=12):
    return pl.pallas_call(
        kernel,
        out_shape=[jax.ShapeDtypeStruct(s, t) for s, t in out_shape],
        in_specs=[SMEM] + [VMEM] * len(args),
        out_specs=[VMEM] * len(out_shape),
        scratch_shapes=list(scratch),
        compiler_params=pltpu.CompilerParams(vmem_limit_bytes=limit * 2**20),
        name=name,
    )(scalars, *args)


def in_hbm(x):
    return pltpu.with_memory_space_constraint(x, pltpu.HBM)


def split3(x):
    high = x.astype(BF16)
    rest = x - high.astype(F32)
    mid = rest.astype(BF16)
    return high, mid, (rest - mid.astype(F32)).astype(BF16)


def dot(a, b):
    return jnp.dot(a, b, preferred_element_type=F32)


def dot_t(a, b):
    return lax.dot_general(a, b, (((1,), (1,)), ((), ())), preferred_element_type=F32)


def dot_exact(a, x):
    out = dot(a, jnp.concatenate(split3(x), axis=1))
    width = x.shape[1]
    return out[:, 0:width] + out[:, width : 2 * width] + out[:, 2 * width :]


def iota(shape, dim):
    return lax.broadcasted_iota(jnp.int32, shape, dim)


def layers(extra):
    return [(1, 0), (GROUP, BUNDLE)] if extra else [(1, 0)]


def bundle_rows(extra):
    return BUNDLE + BUNDLE // GROUP if extra else BUNDLE


def put(ref, at, pieces):
    for piece in pieces:
        ref[at : at + piece.shape[0], :] = piece
        at += piece.shape[0]


def put_pair(ref_a, ref_b, at, parity, plus, minus):
    even = parity == 0
    put(ref_a, at, [jnp.where(even, p, m) for p, m in zip(plus, minus)])
    put(ref_b, at, [jnp.where(even, m, p) for p, m in zip(plus, minus)])


def received(ref_a, ref_b, parity, scale, base):
    even = parity == 0
    rows = ref_b.shape[0]
    paired = ref_a.shape[0] > rows

    def cut(ref, a, b, shift=0):
        return ref[shift + base + a // scale : shift + base + b // scale, :]

    def up(a, b):
        return jnp.where(even, cut(ref_b, a, b), cut(ref_a, a, b))

    def down(a, b):
        return jnp.where(even, cut(ref_a, a, b, rows if paired else 0), cut(ref_b, a, b))

    return up, down


def send_x(parity, values, send_a, send_b, extra):
    for value, (scale, base) in zip(values, layers(extra)):
        width = BUNDLE // scale
        put_pair(send_a, send_b, base, parity, [value[0:width, :]], [value[width : 2 * width, :]])


def route_y(extra, sc, *refs):
    count = 2 if extra else 1
    values, (xa, xb, ya, yb) = refs[:count], refs[count:]
    for value, (scale, base) in zip(values, layers(extra)):
        up, down = received(xa, xb, sc[0], scale, base)
        plus = [up(0, 32), down(0, 32), value[448 // scale : 608 // scale, :]]
        minus = [up(32, 64), down(32, 64), value[608 // scale : 768 // scale, :]]
        put_pair(ya, yb, base, sc[1], plus, minus)


def route_z(extra, sc, *refs):
    count = 2 if extra else 1
    values, (xa, xb, ya, yb, za, zb) = refs[:count], refs[count:]
    for value, (scale, base) in zip(values, layers(extra)):
        x_up, x_down = received(xa, xb, sc[0], scale, base)
        y_up, y_down = received(ya, yb, sc[1], scale, base)
        both = []
        for x_at, y_at, own in ((64, (0, 32, 64), 768), (80, (8, 40, 80), 896)):
            pieces = [x_up(x_at, x_at + EDGE), x_down(x_at, x_at + EDGE)]
            for y in (y_up, y_down):
                for at, width in zip(y_at, (CORNER, CORNER, EDGE)):
                    pieces.append(y(at, at + width))
            pieces.append(value[own // scale : (own + FACE) // scale, :])
            both.append(pieces)
        put_pair(za, zb, base, sc[2], both[0], both[1])


def partner_pieces(sc, xa, xb, ya, yb, za, zb, scale, base):
    x_up, x_down = received(xa, xb, sc[0], scale, base)
    y_up, y_down = received(ya, yb, sc[1], scale, base)
    z_up, z_down = received(za, zb, sc[2], scale, base)
    pieces = []
    for (o1, o2, o3), _, width in SLOTS:
        s1, s2, s3 = -o1, -o2, -o3
        if s3:
            reader = z_up if s3 == 1 else z_down
            if s2:
                at = 32 if s2 == 1 else 64
                at += {1: 0, -1: CORNER, 0: 2 * CORNER}[s1]
            elif s1:
                at = 0 if s1 == 1 else EDGE
            else:
                at = 96
        elif s2:
            reader = y_up if s2 == 1 else y_down
            at = {1: EDGE, -1: 32 + EDGE, 0: 96}[s1]
        else:
            reader = x_up if s1 == 1 else x_down
            at = 96
        pieces.append(reader(at, at + width))
    return pieces


def pack_kernel(sc, order, load, modes, sel_ref, load_ref, comp_ref, mode, row_ref, xa, xb, col, buf, mbuf, sems):
    copy = pltpu.make_async_copy(load, buf, sems.at[0])
    copy.start()
    copy_modes = pltpu.make_async_copy(modes, mbuf, sems.at[1])
    copy_modes.start()
    for offset, begin, width in SLOTS:
        col[OURS[offset] : OURS[offset] + width, :] = order[begin : begin + width, :]
    step = 256
    for at in range(0, ROWS, step):
        lanes = iota((step, ROWS), 1)
        sel_ref[at : at + step, :] = jnp.where(col[at : at + step, :] == lanes, 1.0, 0.0).astype(BF16)
    lane = iota((8, ROWS), 1)
    digits = jnp.where(iota((8, ROWS), 0) == 0, lane // 256, jnp.where(iota((8, ROWS), 0) == 1, lane % 256, 0))
    copy_modes.wait()
    top = jnp.concatenate([mbuf[...].astype(F32), jnp.zeros((8 - NMODE, ROWS), F32)], axis=0)
    mode[...] = jnp.concatenate([top, digits.astype(F32)], axis=0).astype(BF16)
    sel = sel_ref[...]
    rows = dot_t(mode[...], sel)
    row_ref[...] = (rows[8:9, :] * 256.0 + rows[9:10, :]).astype(jnp.int32)
    cols = dot_t(sel, mode[...]).astype(BF16)
    spread = jnp.where(iota((16, 128), 0) == iota((16, 128), 1) % 16, 1.0, 0.0).astype(BF16)
    wide = dot(cols, spread)
    keep = iota((ROWS, 128), 0) % GROUP == iota((ROWS, 128), 1) // 16
    wide = jnp.where(keep, wide, 0.0).astype(BF16)
    fold = jnp.where(iota((ROWS // GROUP, ROWS), 0) == iota((ROWS // GROUP, ROWS), 1) // GROUP, 1.0, 0.0)
    comp_ref[...] = dot(fold.astype(BF16), wide)
    copy.wait()
    load_ref[...] = dot(sel, buf[...])
    send_x(sc[0], (load_ref, comp_ref), xa, xb, True)


def permute_kernel(sel, mode, order_row, dual, out, inv_ref, bt_ref, cols_ref, buf, sem):
    copy = pltpu.make_async_copy(dual, buf, sem)
    copy.start()
    step = 256
    for at in range(0, ROWS, step):
        subs = iota((step, ROWS), 0) + at
        inv_ref[at : at + step, :] = jnp.where(order_row[...] == subs, 1.0, 0.0).astype(BF16)
    bt_ref[...] = dot(mode[...], inv_ref[...]).astype(BF16)
    cols_ref[...] = dot_t(sel[...], mode[...]).astype(BF16)
    copy.wait()
    for at in range(0, ROWS, step):
        rows = dot(sel[at : at + step, :], buf[...]).astype(BF16)
        out[at : at + step, :] = dot(rows, inv_ref[...]).astype(BF16)


def project(sc, bt, residual, out):
    block = dot_exact(bt[...], residual)[0:8, :]
    count = sc[4].astype(F32)
    block = jnp.where(iota((8, 128), 0) == NMODE, count, block)
    for t in range(out.shape[0]):
        out[t, :, :] = block


def first_kernel(sc, load, bt, xa, xb, ya, yb, za, zb, res_ref, comp_ref, out):
    pieces = partner_pieces(sc, xa, xb, ya, yb, za, zb, 1, 0)
    at = 0
    for piece in pieces:
        end = at + piece.shape[0]
        res_ref[at:end, :] = load[at:end, :] + piece
        at = end
    project(sc, bt, res_ref[...], out)
    put(comp_ref, 0, partner_pieces(sc, xa, xb, ya, yb, za, zb, GROUP, BUNDLE))


def next_residual(sc, res, val, bundles, out):
    at = 0
    for piece in partner_pieces(sc, *bundles, 1, 0):
        end = at + piece.shape[0]
        out[at:end, :] = res[at:end, :] - (val[at:end, :] + piece)
        at = end


def step_kernel(sc, res, val, bt, xa, xb, ya, yb, za, zb, res_ref, out):
    next_residual(sc, res, val, (xa, xb, ya, yb, za, zb), res_ref)
    project(sc, bt, res_ref[...], out)


def last_kernel(sc, res, val, inv, xa, xb, ya, yb, za, zb, out, scratch):
    next_residual(sc, res, val, (xa, xb, ya, yb, za, zb), scratch)
    out[...] = dot_exact(inv[...], scratch[...])


def unpack_kernel(sc, inv, val, out):
    out[...] = dot_exact(inv[...], val[...])


def mode_kernel(sc, cols, comp, block, out):
    pick = jnp.where(iota((ROWS, 128), 0) // GROUP == iota((ROWS, 128), 1), 1.0, 0.0).astype(BF16)
    wide = dot(pick, comp[...].astype(BF16))
    keep = iota((ROWS, 128), 0) % GROUP == iota((ROWS, 128), 1) // 16
    wide = jnp.where(keep, wide, 0.0).astype(BF16)
    mode = iota((128, 256), 0) % 16
    fold = jnp.where((mode == iota((128, 256), 1) % 8) & (mode < NMODE), 1.0, 0.0).astype(BF16)
    theirs = dot(wide, fold)
    mode = iota((16, 256), 0)
    own = jnp.where((mode == iota((16, 256), 1) % 8) & (mode < NMODE), 1.0, 0.0).astype(BF16)
    mine = dot(cols[...], own)
    x_even, y_even = sc[0] == 0, sc[1] == 0
    which = jnp.where(
        x_even,
        jnp.where(y_even, block[:, 0:1], block[:, 1:2]),
        jnp.where(y_even, block[:, 2:3], block[:, 3:4]),
    )
    at = iota((ROWS, 256), 1) // 8
    home = 9 * sc[0] + 3 * sc[1] + 1
    out[...] = (jnp.where(at == which, theirs, 0.0) + jnp.where(at == home, mine, 0.0)).astype(BF16)


def line_kernel(sc, line, inverse, mat_ref, out):
    everyone = line[...]
    size, coarse = everyone.shape[0], inverse.shape[0]

    def selection(rows, first):
        row = iota((rows, size), 0) + first
        col = iota((rows, size), 1)
        is_count = col % 8 == NMODE
        here = jnp.where(is_count & (col // 8 == row // 8), 1.0, 0.0)
        before = jnp.where(is_count & (col // 8 < row // 8), 1.0, 0.0)
        count = jnp.dot(here, everyone, precision=HIGHEST, preferred_element_type=F32)
        offset = jnp.dot(before, everyone, precision=HIGHEST, preferred_element_type=F32)
        mode = ((iota((rows, 128), 0) + first) % 8).astype(F32)
        compact = iota((rows, 128), 1).astype(F32)
        hit = (compact == offset + mode) & (mode < count)
        return jnp.where(hit, 1.0, 0.0)[:, 0:coarse]

    everywhere = selection(size, 0)
    near = selection(24, 8 * sc[3] - 8)
    rows = jnp.dot(near, inverse[...], precision=HIGHEST, preferred_element_type=F32)
    matrix = lax.dot_general(rows, everywhere, (((1,), (1,)), ((), ())), precision=HIGHEST, preferred_element_type=F32)
    mat_ref[...] = matrix
    out[...] = jnp.dot(matrix, everyone, precision=HIGHEST, preferred_element_type=F32)


def solve_kernel(sc, line, matrix, out):
    out[...] = jnp.dot(matrix[...], line[...], precision=HIGHEST, preferred_element_type=F32)


def advance_kernel(keep, take, sc, *refs):
    if keep:
        res, modes, dual, xa, xb, old_dir, old_mul, dir_ref, mul_ref, val_ref, sa, sb, stack = refs
    else:
        res, modes, dual, xa, xb, dir_ref, val_ref, sa, sb, stack = refs
    put(stack, 0, [xa[...], xb[...], jnp.zeros((40, 128), F32)])
    corrected = res[...] - dot_exact(modes[...], stack[...])
    if keep:
        direction = keep * old_dir[...] + take * corrected
        mul_ref[...] = old_mul[...] + direction
    else:
        direction = corrected / take
    dir_ref[...] = direction
    val_ref[...] = dot(dual[...], direction.astype(BF16))
    send_x(sc[0], (val_ref,), sa, sb, False)


def label(sign, odd):
    if sign == 0:
        return odd
    return 1 - odd if (sign == 1) != odd else 2


def amplitude_blocks():
    out = np.zeros((ROWS, 4), np.int32)
    for x_odd in (0, 1):
        for y_odd in (0, 1):
            for (o1, o2, o3), _, width in SLOTS:
                at = OURS[(o1, o2, o3)]
                block = 3 * (3 * label(o1, x_odd) + label(o2, y_odd)) + o3 + 1
                out[at : at + width, 2 * x_odd + y_odd] = block
    return out


def cross(sc, values, x, extra):
    rows = bundle_rows(extra)
    pair = [((rows, 128), F32)] * 2
    y = exchange(*call(functools.partial(route_y, extra), pair, sc, *values, *x, name="route_y"), "gy")
    z = exchange(*call(functools.partial(route_z, extra), pair, sc, *values, *x, *y, name="route_z"), "gz")
    return (*x, *y, *z)


def local(dual_blocks, load_terms, row_order, mode_rows, mode_count, coarse_inverse):
    line_length = lax.axis_size("gz")
    pos = [lax.axis_index(axis) for axis in ("gx", "gy", "gz")]
    sc = jnp.stack([p % 2 for p in pos] + [pos[2], mode_count[0, 0, 0]]).astype(jnp.int32)
    inverse = coarse_inverse[0, 0]
    bundle = [((BUNDLE, 128), F32)] * 2
    vector = ((ROWS, 128), F32)
    square = ((ROWS, ROWS), BF16)
    wide = [((bundle_rows(True), 128), F32)] * 2
    gathered = ((line_length, 8, 128), F32)

    sel, load_rows, comp, mode, order_row, sa, sb = pl.pallas_call(
        pack_kernel,
        out_shape=[
            jax.ShapeDtypeStruct(*v)
            for v in (
                square,
                vector,
                ((ROWS // GROUP, 128), F32),
                ((16, ROWS), BF16),
                ((1, ROWS), jnp.int32),
                *wide,
            )
        ],
        in_specs=[SMEM, VMEM, HBM, HBM],
        out_specs=[VMEM] * 7,
        scratch_shapes=[
            pltpu.VMEM((ROWS, 1), jnp.int32),
            pltpu.VMEM((ROWS, 128), BF16),
            pltpu.VMEM((NMODE, ROWS), BF16),
            pltpu.SemaphoreType.DMA((2,)),
        ],
        compiler_params=pltpu.CompilerParams(vmem_limit_bytes=16 * 2**20),
        name="pack",
    )(sc, row_order[0, 0, 0][:, None], in_hbm(load_terms[0, 0, 0]), in_hbm(mode_rows[0, 0, 0].T))
    x = exchange_async(sa, sb, "gx")
    dual, inv, bt, cols = pl.pallas_call(
        permute_kernel,
        out_shape=[jax.ShapeDtypeStruct(*v) for v in (square, square, ((16, ROWS), BF16), ((ROWS, 16), BF16))],
        in_specs=[VMEM, VMEM, VMEM, HBM],
        out_specs=[VMEM] * 4,
        scratch_shapes=[pltpu.VMEM((ROWS, ROWS), BF16), pltpu.SemaphoreType.DMA],
        compiler_params=pltpu.CompilerParams(vmem_limit_bytes=16 * 2**20),
        name="permute",
    )(sel, mode, order_row, in_hbm(dual_blocks[0, 0, 0]))
    *x, dual, inv, bt, cols = lax.optimization_barrier((*x, dual, inv, bt, cols))
    received_rows = cross(sc, (load_rows, comp), x, True)
    residual, their_comp, proj = call(
        first_kernel,
        [vector, ((ROWS // GROUP, 128), F32), gathered],
        sc,
        load_rows,
        bt,
        *received_rows,
        name="first",
    )
    (modes_near,) = call(
        mode_kernel, [((ROWS, 256), BF16)], sc, cols, their_comp, jnp.asarray(amplitude_blocks()), name="modes"
    )

    center_value = 0.5 * (EIG_HIGH + EIG_LOW)
    half_width = 0.5 * (EIG_HIGH - EIG_LOW)
    rho_prev = half_width / center_value
    amp = ((24, 128), F32)
    for iteration in range(ITERS):
        line = lax.all_to_all(proj, "gz", 0, 0, tiled=True).reshape(8 * line_length, 128)
        if iteration == 0:
            matrix, own = call(line_kernel, [((24, 8 * line_length), F32), amp], sc, line, inverse, name="line")
        else:
            (own,) = call(solve_kernel, [amp], sc, line, matrix, name="solve")
        column = jnp.concatenate(exchange(own, own, "gy"), axis=0)
        near = (modes_near, dual, *exchange(column, column, "gx"))
        scratch = [pltpu.VMEM((256, 128), F32)]
        if iteration == 0:
            direction, value, sa, sb = call(
                functools.partial(advance_kernel, None, center_value),
                [vector, vector, *bundle],
                sc,
                residual,
                *near,
                scratch=scratch,
                name="advance0",
            )
            multipliers = direction
        else:
            rho_now = 1.0 / (2.0 * center_value / half_width - rho_prev)
            direction, multipliers, value, sa, sb = call(
                functools.partial(advance_kernel, rho_now * rho_prev, 2.0 * rho_now / half_width),
                [vector, vector, vector, *bundle],
                sc,
                residual,
                *near,
                direction,
                multipliers,
                scratch=scratch,
                name="advance",
            )
            rho_prev = rho_now
        received_rows = cross(sc, (value,), exchange(sa, sb, "gx"), False)
        if iteration < ITERS - 1:
            residual, proj = call(
                step_kernel, [vector, gathered], sc, residual, value, bt, *received_rows, name="step"
            )
    (out_mul,) = call(unpack_kernel, [vector], sc, inv, multipliers, name="unpack")
    (out_res,) = call(
        last_kernel,
        [vector],
        sc,
        residual,
        value,
        inv,
        *received_rows,
        scratch=[pltpu.VMEM((ROWS, 128), F32)],
        name="last",
    )
    return out_mul[None, None, None], out_res[None, None, None]


def solution(mesh):
    in_specs = (
        P("gx", "gy", "gz", None, None),
        P("gx", "gy", "gz", None, None),
        P("gx", "gy", "gz", None),
        P("gx", "gy", "gz", None, None),
        P("gx", "gy", "gz"),
        P("gx", "gy", None, None),
    )
    out_specs = (P("gx", "gy", "gz", None, None), P("gx", "gy", "gz", None, None))
    return jax.shard_map(local, mesh=mesh, in_specs=in_specs, out_specs=out_specs, check_vma=False)
```

```python
import functools

import jax
import jax.numpy as jnp
import numpy as np
from jax import lax
from jax.experimental import pallas as pl
from jax.experimental.pallas import tpu as pltpu
from jax.sharding import PartitionSpec as P

FACE = 128
EDGE = 16
CORNER = 8
NMODE = 6
ITERS = 3
EIG_LOW = 0.5
EIG_HIGH = 6.0

F32 = jnp.float32
BF16 = jnp.bfloat16
HIGHEST = lax.Precision.HIGHEST
SIGNS = (1, -1, 0)
WIDTHS = {1: FACE, 2: EDGE, 3: CORNER}

BUNDLE = 224
NEAR = 32
STACK = 16 * NEAR
GROUP = 8


def tables():
    begin, row = {}, 0
    for weight in (1, 2, 3):
        for o1 in (-1, 0, 1):
            for o2 in (-1, 0, 1):
                for o3 in (-1, 0, 1):
                    if abs(o1) + abs(o2) + abs(o3) == weight:
                        begin[(o1, o2, o3)] = row
                        row += WIDTHS[weight]
    slots, ours, row = [], {}, 0
    for o1 in SIGNS:
        for o2 in SIGNS:
            for o3 in SIGNS:
                offset = (o1, o2, o3)
                if any(offset):
                    width = WIDTHS[abs(o1) + abs(o2) + abs(o3)]
                    slots.append((offset, begin[offset], width))
                    ours[offset] = row
                    row += width
    return slots, ours, row


SLOTS, OURS, ROWS = tables()


def swaps(size, parity):
    pairs = [(i, i + 1) for i in range(parity, size - 1, 2)]
    return pairs + [(j, i) for i, j in pairs]


def exchange(first, second, axis):
    size = lax.axis_size(axis)
    groups = [[i, i + 1] for i in range(0, size, 2)]
    other = lax.ppermute(second, axis, swaps(size, 1))
    return lax.all_gather(first, axis, axis_index_groups=groups, tiled=True), other


def exchange_async(first, second, axis):
    size = lax.axis_size(axis)
    return lax.ppermute(first, axis, swaps(size, 0)), lax.ppermute(second, axis, swaps(size, 1))


VMEM = pl.BlockSpec(memory_space=pltpu.VMEM)
HBM = pl.BlockSpec(memory_space=pltpu.HBM)
SMEM = pl.BlockSpec(memory_space=pltpu.SMEM)


def call(kernel, out_shape, scalars, *args, scratch=(), name=None, limit=12):
    return pl.pallas_call(
        kernel,
        out_shape=[jax.ShapeDtypeStruct(s, t) for s, t in out_shape],
        in_specs=[SMEM] + [VMEM] * len(args),
        out_specs=[VMEM] * len(out_shape),
        scratch_shapes=list(scratch),
        compiler_params=pltpu.CompilerParams(vmem_limit_bytes=limit * 2**20),
        name=name,
    )(scalars, *args)


def in_hbm(x):
    return pltpu.with_memory_space_constraint(x, pltpu.HBM)


def dot(a, b):
    return jnp.dot(a, b, preferred_element_type=F32)


def dot_t(a, b):
    return lax.dot_general(a, b, (((1,), (1,)), ((), ())), preferred_element_type=F32)


def dot_wide(a, x):
    high = x.astype(BF16)
    low = (x - high.astype(F32)).astype(BF16)
    out = dot(a, jnp.concatenate([high, low], axis=1))
    width = x.shape[1]
    return out[:, 0:width] + out[:, width:]


def iota(shape, dim):
    return lax.broadcasted_iota(jnp.int32, shape, dim)


def layers(extra):
    return [(1, 0), (GROUP, BUNDLE)] if extra else [(1, 0)]


def bundle_rows(extra):
    return BUNDLE + 32 if extra else BUNDLE


def put(ref, at, pieces):
    for piece in pieces:
        ref[at : at + piece.shape[0], :] = piece
        at += piece.shape[0]


def put_pair(ref_a, ref_b, at, parity, plus, minus):
    even = parity == 0
    put(ref_a, at, [jnp.where(even, p, m) for p, m in zip(plus, minus)])
    put(ref_b, at, [jnp.where(even, m, p) for p, m in zip(plus, minus)])


def received(ref_a, ref_b, parity, scale, base):
    even = parity == 0
    rows = ref_b.shape[0]
    paired = ref_a.shape[0] > rows

    def cut(ref, a, b, shift=0):
        return ref[shift + base + a // scale : shift + base + b // scale, :]

    def up(a, b):
        return jnp.where(even, cut(ref_b, a, b), cut(ref_a, a, b))

    def down(a, b):
        return jnp.where(even, cut(ref_a, a, b, rows if paired else 0), cut(ref_b, a, b))

    return up, down


def blank(extra, *refs):
    if extra:
        for ref in refs:
            ref[bundle_rows(extra) - 8 :, :] = jnp.zeros((8, 128), F32)


def send_x(parity, values, send_a, send_b, extra):
    blank(extra, send_a, send_b)
    for value, (scale, base) in zip(values, layers(extra)):
        width = BUNDLE // scale
        put_pair(send_a, send_b, base, parity, [value[0:width, :]], [value[width : 2 * width, :]])


def route_y(extra, sc, *refs):
    count = 2 if extra else 1
    values, (xa, xb, ya, yb) = refs[:count], refs[count:]
    blank(extra, ya, yb)
    for value, (scale, base) in zip(values, layers(extra)):
        up, down = received(xa, xb, sc[0], scale, base)
        plus = [up(0, 32), down(0, 32), value[448 // scale : 608 // scale, :]]
        minus = [up(32, 64), down(32, 64), value[608 // scale : 768 // scale, :]]
        put_pair(ya, yb, base, sc[1], plus, minus)


def route_z(extra, sc, *refs):
    count = 2 if extra else 1
    values, (xa, xb, ya, yb, za, zb) = refs[:count], refs[count:]
    blank(extra, za, zb)
    for value, (scale, base) in zip(values, layers(extra)):
        x_up, x_down = received(xa, xb, sc[0], scale, base)
        y_up, y_down = received(ya, yb, sc[1], scale, base)
        both = []
        for x_at, y_at, own in ((64, (0, 32, 64), 768), (80, (8, 40, 80), 896)):
            pieces = [x_up(x_at, x_at + EDGE), x_down(x_at, x_at + EDGE)]
            for y in (y_up, y_down):
                for at, width in zip(y_at, (CORNER, CORNER, EDGE)):
                    pieces.append(y(at, at + width))
            pieces.append(value[own // scale : (own + FACE) // scale, :])
            both.append(pieces)
        put_pair(za, zb, base, sc[2], both[0], both[1])


def partner_pieces(sc, xa, xb, ya, yb, za, zb, scale, base):
    x_up, x_down = received(xa, xb, sc[0], scale, base)
    y_up, y_down = received(ya, yb, sc[1], scale, base)
    z_up, z_down = received(za, zb, sc[2], scale, base)
    pieces = []
    for (o1, o2, o3), _, width in SLOTS:
        s1, s2, s3 = -o1, -o2, -o3
        if s3:
            reader = z_up if s3 == 1 else z_down
            if s2:
                at = 32 if s2 == 1 else 64
                at += {1: 0, -1: CORNER, 0: 2 * CORNER}[s1]
            elif s1:
                at = 0 if s1 == 1 else EDGE
            else:
                at = 96
        elif s2:
            reader = y_up if s2 == 1 else y_down
            at = {1: EDGE, -1: 32 + EDGE, 0: 96}[s1]
        else:
            reader = x_up if s1 == 1 else x_down
            at = 96
        pieces.append(reader(at, at + width))
    return pieces


def pack_kernel(sc, order, load, modes, sel_ref, load_ref, comp_ref, mode, cols_ref, xa, xb, col, buf, mbuf, sems):
    copy = pltpu.make_async_copy(load, buf, sems.at[0])
    copy.start()
    copy_modes = pltpu.make_async_copy(modes, mbuf, sems.at[1])
    copy_modes.start()
    for offset, begin, width in SLOTS:
        col[OURS[offset] : OURS[offset] + width, :] = order[begin : begin + width, :]
    step = 256
    for at in range(0, ROWS, step):
        lanes = iota((step, ROWS), 1)
        sel_ref[at : at + step, :] = jnp.where(col[at : at + step, :] == lanes, 1.0, 0.0).astype(BF16)
    copy_modes.wait()
    top = jnp.concatenate([mbuf[...].astype(F32), jnp.zeros((16 - NMODE, ROWS), F32)], axis=0)
    mode[...] = top.astype(BF16)
    sel = sel_ref[...]
    cols = dot_t(sel, mode[...]).astype(BF16)
    cols_ref[...] = cols
    spread = jnp.where(iota((16, 128), 0) == iota((16, 128), 1) % 16, 1.0, 0.0).astype(BF16)
    wide = dot(cols, spread)
    keep = iota((ROWS, 128), 0) % GROUP == iota((ROWS, 128), 1) // 16
    wide = jnp.where(keep, wide, 0.0).astype(BF16)
    fold = jnp.where(iota((ROWS // GROUP, ROWS), 0) == iota((ROWS // GROUP, ROWS), 1) // GROUP, 1.0, 0.0)
    comp_ref[...] = dot(fold.astype(BF16), wide)
    copy.wait()
    load_ref[...] = dot(sel, buf[...])
    send_x(sc[0], (load_ref, comp_ref), xa, xb, True)


def permute_kernel(sel, mode, order_row, dual, out, inv_ref, bt_ref, buf, sem):
    copy = pltpu.make_async_copy(dual, buf, sem)
    copy.start()
    packed = jnp.concatenate([order_row[:, begin : begin + width] for _, begin, width in SLOTS], axis=1)
    step = 256
    for at in range(0, ROWS, step):
        subs = iota((step, ROWS), 0) + at
        inv_ref[at : at + step, :] = jnp.where(packed == subs, 1.0, 0.0).astype(BF16)
    bt_ref[...] = dot(mode[...], inv_ref[...]).astype(BF16)
    copy.wait()
    for at in range(0, out.shape[0], step):
        rows = dot(sel[at : at + step, :], buf[...]).astype(BF16)
        out[at : at + step, :] = dot(rows, inv_ref[...]).astype(BF16)


def permute_rest_kernel(first, sel, inv, dual, out):
    step = 256
    for at in range(0, out.shape[0], step):
        rows = dot(sel[first + at : first + at + step, :], dual[...]).astype(BF16)
        out[at : at + step, :] = dot(rows, inv[...]).astype(BF16)


def project(sc, bt, residual, out):
    block = dot_wide(bt[...], residual)[0:8, :]
    count = sc[4].astype(F32)
    block = jnp.where(iota((8, 128), 0) == NMODE, count, block)
    for t in range(out.shape[0]):
        out[t, :, :] = block


def first_kernel(sc, load, bt, xa, xb, ya, yb, za, zb, res_ref, comp_ref, out):
    pieces = partner_pieces(sc, xa, xb, ya, yb, za, zb, 1, 0)
    at = 0
    for piece in pieces:
        end = at + piece.shape[0]
        res_ref[at:end, :] = load[at:end, :] + piece
        at = end
    project(sc, bt, res_ref[...], out)
    put(comp_ref, 0, partner_pieces(sc, xa, xb, ya, yb, za, zb, GROUP, BUNDLE))


def next_residual(sc, res, val, bundles, out):
    at = 0
    for piece in partner_pieces(sc, *bundles, 1, 0):
        end = at + piece.shape[0]
        out[at:end, :] = res[at:end, :] - (val[at:end, :] + piece)
        at = end


def step_kernel(sc, res, val, bt, xa, xb, ya, yb, za, zb, res_ref, out):
    next_residual(sc, res, val, (xa, xb, ya, yb, za, zb), res_ref)
    project(sc, bt, res_ref[...], out)


def last_kernel(sc, res, val, inv, xa, xb, ya, yb, za, zb, out, scratch):
    next_residual(sc, res, val, (xa, xb, ya, yb, za, zb), scratch)
    out[...] = dot_wide(inv[...], scratch[...])


def unpack_kernel(sc, inv, val, out):
    out[...] = dot_wide(inv[...], val[...])


def mode_kernel(sc, cols, comp, block, out):
    pick = jnp.where(iota((ROWS, 128), 0) // GROUP == iota((ROWS, 128), 1), 1.0, 0.0).astype(BF16)
    wide = dot(pick, comp[...].astype(BF16))
    keep = iota((ROWS, 128), 0) % GROUP == iota((ROWS, 128), 1) // 16
    wide = jnp.where(keep, wide, 0.0).astype(BF16)
    mode = iota((128, STACK), 0) % 16
    fold = jnp.where((mode == iota((128, STACK), 1) % 8) & (mode < NMODE), 1.0, 0.0).astype(BF16)
    theirs = dot(wide, fold)
    mode = iota((16, STACK), 0)
    own = jnp.where((mode == iota((16, STACK), 1) % 8) & (mode < NMODE), 1.0, 0.0).astype(BF16)
    mine = dot(cols[...], own)
    x_even, y_even = sc[0] == 0, sc[1] == 0
    which = jnp.where(
        x_even,
        jnp.where(y_even, block[:, 0:1], block[:, 1:2]),
        jnp.where(y_even, block[:, 2:3], block[:, 3:4]),
    )
    which = which + sc[2]
    at = iota((ROWS, STACK), 1) // 8
    home = 16 * sc[0] + 4 * sc[1] + 1 + sc[2]
    out[...] = (jnp.where(at == which, theirs, 0.0) + jnp.where(at == home, mine, 0.0)).astype(BF16)


def line_kernel(sc, line, inverse, mat_ref, out, buf, sem):
    copy = pltpu.make_async_copy(inverse, buf, sem)
    copy.start()
    everyone = line[...]
    size, coarse = everyone.shape[0], inverse.shape[0]

    def selection(rows, first):
        row = iota((rows, size), 0) + first
        col = iota((rows, size), 1)
        is_count = col % 8 == NMODE
        here = jnp.where(is_count & (col // 8 == row // 8), 1.0, 0.0)
        before = jnp.where(is_count & (col // 8 < row // 8), 1.0, 0.0)
        count = jnp.dot(here, everyone, precision=HIGHEST, preferred_element_type=F32)
        offset = jnp.dot(before, everyone, precision=HIGHEST, preferred_element_type=F32)
        mode = ((iota((rows, 128), 0) + first) % 8).astype(F32)
        compact = iota((rows, 128), 1).astype(F32)
        hit = (compact == offset + mode) & (mode < count)
        return jnp.where(hit, 1.0, 0.0)[:, 0:coarse]

    everywhere = selection(size, 0)
    near = selection(NEAR, 8 * (sc[3] - sc[2]) - 8)
    copy.wait()
    rows = jnp.dot(near, buf[...], precision=HIGHEST, preferred_element_type=F32)
    matrix = lax.dot_general(rows, everywhere, (((1,), (1,)), ((), ())), precision=HIGHEST, preferred_element_type=F32)
    mat_ref[...] = matrix
    out[...] = jnp.dot(matrix, everyone, precision=HIGHEST, preferred_element_type=F32)


def solve_kernel(sc, line, matrix, out):
    out[...] = jnp.dot(matrix[...], line[...], precision=HIGHEST, preferred_element_type=F32)


def advance_kernel(keep, take, sc, *refs):
    if keep:
        res, modes, dual_a, dual_b, stack, old_dir, old_mul, dir_ref, mul_ref, val_ref, sa, sb = refs
    else:
        res, modes, dual_a, dual_b, stack, dir_ref, val_ref, sa, sb = refs
    corrected = res[...] - dot_wide(modes[...], stack[...])
    if keep:
        direction = keep * old_dir[...] + take * corrected
        mul_ref[...] = old_mul[...] + direction
    else:
        direction = corrected / take
    dir_ref[...] = direction
    rounded = direction.astype(BF16)
    val_ref[0 : ROWS // 2, :] = dot(dual_a[...], rounded)
    val_ref[ROWS // 2 :, :] = dot(dual_b[...], rounded)
    send_x(sc[0], (val_ref,), sa, sb, False)


def share(block, axis):
    size, line = lax.axis_size(axis), lax.axis_size("gz")
    groups = []
    for z in range(line):
        for even in range(0, size, 2):
            odd = (even + 1 if z % 2 == 0 else even - 1) % size
            groups.append([even * line + z, odd * line + z])
    block = lax.all_gather(block, (axis, "gz"), axis_index_groups=groups, tiled=True)
    return lax.all_gather(block, "gz", axis_index_groups=[[z, z + 1] for z in range(0, line, 2)], tiled=True)


def label(sign, odd):
    if sign == 0:
        return odd
    if odd:
        return 2 if sign == 1 else 0
    return 1 if sign == 1 else 3


def amplitude_blocks():
    out = np.zeros((ROWS, 4), np.int32)
    for x_odd in (0, 1):
        for y_odd in (0, 1):
            for (o1, o2, o3), _, width in SLOTS:
                at = OURS[(o1, o2, o3)]
                block = 4 * (4 * label(o1, x_odd) + label(o2, y_odd)) + o3 + 1
                out[at : at + width, 2 * x_odd + y_odd] = block
    return out


def cross(sc, value, x):
    pair = [((BUNDLE, 128), F32)] * 2
    y = exchange(*call(functools.partial(route_y, False), pair, sc, value, *x, name="route_y"), "gy")
    z = exchange(*call(functools.partial(route_z, False), pair, sc, value, *x, *y, name="route_z"), "gz")
    return (*x, *y, *z)


def local(dual_blocks, load_terms, row_order, mode_rows, mode_count, coarse_inverse):
    line_length = lax.axis_size("gz")
    pos = [lax.axis_index(axis) for axis in ("gx", "gy", "gz")]
    sc = jnp.stack([p % 2 for p in pos] + [pos[2], mode_count[0, 0, 0]]).astype(jnp.int32)
    inverse = in_hbm(coarse_inverse[0, 0])
    bundle = [((BUNDLE, 128), F32)] * 2
    vector = ((ROWS, 128), F32)
    square = ((ROWS, ROWS), BF16)
    wide = [((bundle_rows(True), 128), F32)] * 2
    gathered = ((line_length, 8, 128), F32)

    sel, load_rows, comp, mode, cols, sa, sb = pl.pallas_call(
        pack_kernel,
        out_shape=[
            jax.ShapeDtypeStruct(*v)
            for v in (
                square,
                vector,
                ((ROWS // GROUP, 128), F32),
                ((16, ROWS), BF16),
                ((ROWS, 16), BF16),
                *wide,
            )
        ],
        in_specs=[SMEM, VMEM, HBM, HBM],
        out_specs=[VMEM] * 7,
        scratch_shapes=[
            pltpu.VMEM((ROWS, 1), jnp.int32),
            pltpu.VMEM((ROWS, 128), BF16),
            pltpu.VMEM((NMODE, ROWS), BF16),
            pltpu.SemaphoreType.DMA((2,)),
        ],
        compiler_params=pltpu.CompilerParams(vmem_limit_bytes=16 * 2**20),
        name="pack",
    )(sc, row_order[0, 0, 0][:, None], in_hbm(load_terms[0, 0, 0]), in_hbm(mode_rows[0, 0, 0].T))
    half = ((ROWS // 2, ROWS), BF16)
    x = exchange_async(sa, sb, "gx")
    dual_a, inv, bt = pl.pallas_call(
        permute_kernel,
        out_shape=[jax.ShapeDtypeStruct(*v) for v in (half, square, ((16, ROWS), BF16))],
        in_specs=[VMEM, VMEM, VMEM, HBM],
        out_specs=[VMEM] * 3,
        scratch_shapes=[pltpu.VMEM((ROWS, ROWS), BF16), pltpu.SemaphoreType.DMA],
        compiler_params=pltpu.CompilerParams(vmem_limit_bytes=16 * 2**20),
        name="permute",
    )(sel, mode, row_order[0, 0, 0][None, :], in_hbm(dual_blocks[0, 0, 0]))
    *x, dual_a, inv, bt = lax.optimization_barrier((*x, dual_a, inv, bt))
    values = (load_rows, comp)
    y = exchange_async(*call(functools.partial(route_y, True), wide, sc, *values, *x, name="route_y"), "gy")
    (dual_b,) = pl.pallas_call(
        functools.partial(permute_rest_kernel, ROWS // 2),
        out_shape=[jax.ShapeDtypeStruct(*half)],
        in_specs=[VMEM] * 3,
        out_specs=[VMEM],
        compiler_params=pltpu.CompilerParams(vmem_limit_bytes=12 * 2**20),
        name="permute_rest",
    )(sel, inv, dual_blocks[0, 0, 0])
    *y, dual_b = lax.optimization_barrier((*y, dual_b))
    z = exchange(*call(functools.partial(route_z, True), wide, sc, *values, *x, *y, name="route_z"), "gz")
    received_rows = (*x, *y, *z)
    residual, their_comp, proj = call(
        first_kernel,
        [vector, ((ROWS // GROUP, 128), F32), gathered],
        sc,
        load_rows,
        bt,
        *received_rows,
        name="first",
    )
    center_value = 0.5 * (EIG_HIGH + EIG_LOW)
    half_width = 0.5 * (EIG_HIGH - EIG_LOW)
    rho_prev = half_width / center_value
    amp = ((NEAR, 128), F32)
    for iteration in range(ITERS):
        line = lax.all_to_all(proj, "gz", 0, 0, tiled=True).reshape(8 * line_length, 128)
        if iteration == 0:
            matrix, own = pl.pallas_call(
                line_kernel,
                out_shape=[jax.ShapeDtypeStruct((NEAR, 8 * line_length), F32), jax.ShapeDtypeStruct(*amp)],
                in_specs=[SMEM, VMEM, HBM],
                out_specs=[VMEM] * 2,
                scratch_shapes=[pltpu.VMEM(inverse.shape, F32), pltpu.SemaphoreType.DMA],
                compiler_params=pltpu.CompilerParams(vmem_limit_bytes=12 * 2**20),
                name="line",
            )(sc, line, inverse)
            their_comp, own = lax.optimization_barrier((their_comp, own))
            (modes_near,) = call(
                mode_kernel, [((ROWS, STACK), BF16)], sc, cols, their_comp, jnp.asarray(amplitude_blocks()), name="modes"
            )
        else:
            (own,) = call(solve_kernel, [amp], sc, line, matrix, name="solve")
        near = (modes_near, dual_a, dual_b, share(share(own, "gy"), "gx"))
        if iteration == 0:
            direction, value, sa, sb = call(
                functools.partial(advance_kernel, None, center_value),
                [vector, vector, *bundle],
                sc,
                residual,
                *near,
                name="advance0",
            )
            multipliers = direction
        else:
            rho_now = 1.0 / (2.0 * center_value / half_width - rho_prev)
            direction, multipliers, value, sa, sb = call(
                functools.partial(advance_kernel, rho_now * rho_prev, 2.0 * rho_now / half_width),
                [vector, vector, vector, *bundle],
                sc,
                residual,
                *near,
                direction,
                multipliers,
                name="advance",
            )
            rho_prev = rho_now
        if iteration < ITERS - 1:
            received_rows = cross(sc, value, exchange(sa, sb, "gx"))
            residual, proj = call(
                step_kernel, [vector, gathered], sc, residual, value, bt, *received_rows, name="step"
            )
    x = exchange_async(sa, sb, "gx")
    (out_mul,) = call(unpack_kernel, [vector], sc, inv, multipliers, name="unpack")
    *x, out_mul = lax.optimization_barrier((*x, out_mul))
    received_rows = cross(sc, value, x)
    (out_res,) = call(
        last_kernel,
        [vector],
        sc,
        residual,
        value,
        inv,
        *received_rows,
        scratch=[pltpu.VMEM((ROWS, 128), F32)],
        name="last",
    )
    return out_mul[None, None, None], out_res[None, None, None]


def solution(mesh):
    in_specs = (
        P("gx", "gy", "gz", None, None),
        P("gx", "gy", "gz", None, None),
        P("gx", "gy", "gz", None),
        P("gx", "gy", "gz", None, None),
        P("gx", "gy", "gz"),
        P("gx", "gy", None, None),
    )
    out_specs = (P("gx", "gy", "gz", None, None), P("gx", "gy", "gz", None, None))
    return jax.shard_map(local, mesh=mesh, in_specs=in_specs, out_specs=out_specs, check_vma=False)
```

```python
import functools

import jax
import jax.numpy as jnp
import numpy as np
from jax import lax
from jax.experimental import pallas as pl
from jax.experimental.pallas import tpu as pltpu
from jax.sharding import PartitionSpec as P

FACE = 128
EDGE = 16
CORNER = 8
NMODE = 6
ITERS = 3
EIG_LOW = 0.5
EIG_HIGH = 6.0

F32 = jnp.float32
BF16 = jnp.bfloat16
HIGHEST = lax.Precision.HIGHEST
SIGNS = (1, -1, 0)
WIDTHS = {1: FACE, 2: EDGE, 3: CORNER}

BUNDLE = 224
NEAR = 4 * NMODE
STACK = 16 * NEAR
GROUP = 8


def tables():
    begin, row = {}, 0
    for weight in (1, 2, 3):
        for o1 in (-1, 0, 1):
            for o2 in (-1, 0, 1):
                for o3 in (-1, 0, 1):
                    if abs(o1) + abs(o2) + abs(o3) == weight:
                        begin[(o1, o2, o3)] = row
                        row += WIDTHS[weight]
    slots, ours, row = [], {}, 0
    for o1 in SIGNS:
        for o2 in SIGNS:
            for o3 in SIGNS:
                offset = (o1, o2, o3)
                if any(offset):
                    width = WIDTHS[abs(o1) + abs(o2) + abs(o3)]
                    slots.append((offset, begin[offset], width))
                    ours[offset] = row
                    row += width
    return slots, ours, row


SLOTS, OURS, ROWS = tables()


def swaps(size, parity):
    pairs = [(i, i + 1) for i in range(parity, size - 1, 2)]
    return pairs + [(j, i) for i, j in pairs]


def exchange(first, second, axis):
    size = lax.axis_size(axis)
    groups = [[i, i + 1] for i in range(0, size, 2)]
    other = lax.ppermute(second, axis, swaps(size, 1))
    return lax.all_gather(first, axis, axis_index_groups=groups, tiled=True), other


def exchange_async(first, second, axis):
    size = lax.axis_size(axis)
    return lax.ppermute(first, axis, swaps(size, 0)), lax.ppermute(second, axis, swaps(size, 1))


VMEM = pl.BlockSpec(memory_space=pltpu.VMEM)
HBM = pl.BlockSpec(memory_space=pltpu.HBM)
SMEM = pl.BlockSpec(memory_space=pltpu.SMEM)


def call(kernel, out_shape, scalars, *args, scratch=(), name=None, limit=12):
    return pl.pallas_call(
        kernel,
        out_shape=[jax.ShapeDtypeStruct(s, t) for s, t in out_shape],
        in_specs=[SMEM] + [VMEM] * len(args),
        out_specs=[VMEM] * len(out_shape),
        scratch_shapes=list(scratch),
        compiler_params=pltpu.CompilerParams(vmem_limit_bytes=limit * 2**20),
        name=name,
    )(scalars, *args)


def in_hbm(x):
    return pltpu.with_memory_space_constraint(x, pltpu.HBM)


def dot(a, b):
    return jnp.dot(a, b, preferred_element_type=F32)


def dot_t(a, b):
    return lax.dot_general(a, b, (((1,), (1,)), ((), ())), preferred_element_type=F32)


def dot_wide(a, x):
    high = x.astype(BF16)
    low = (x - high.astype(F32)).astype(BF16)
    out = dot(a, jnp.concatenate([high, low], axis=1))
    width = x.shape[1]
    return out[:, 0:width] + out[:, width:]


def iota(shape, dim):
    return lax.broadcasted_iota(jnp.int32, shape, dim)


def layers(extra):
    return [(1, 0), (GROUP, BUNDLE)] if extra else [(1, 0)]


def bundle_rows(extra):
    return BUNDLE + 32 if extra else BUNDLE


def put(ref, at, pieces):
    for piece in pieces:
        ref[at : at + piece.shape[0], :] = piece
        at += piece.shape[0]


def put_pair(ref_a, ref_b, at, parity, plus, minus):
    even = parity == 0
    put(ref_a, at, [jnp.where(even, p, m) for p, m in zip(plus, minus)])
    put(ref_b, at, [jnp.where(even, m, p) for p, m in zip(plus, minus)])


def received(ref_a, ref_b, parity, scale, base):
    even = parity == 0
    rows = ref_b.shape[0]
    paired = ref_a.shape[0] > rows

    def cut(ref, a, b, shift=0):
        return ref[shift + base + a // scale : shift + base + b // scale, :]

    def up(a, b):
        return jnp.where(even, cut(ref_b, a, b), cut(ref_a, a, b))

    def down(a, b):
        return jnp.where(even, cut(ref_a, a, b, rows if paired else 0), cut(ref_b, a, b))

    return up, down


def blank(extra, *refs):
    if extra:
        for ref in refs:
            ref[bundle_rows(extra) - 8 :, :] = jnp.zeros((8, 128), F32)


def send_x(parity, values, send_a, send_b, extra):
    blank(extra, send_a, send_b)
    for value, (scale, base) in zip(values, layers(extra)):
        width = BUNDLE // scale
        put_pair(send_a, send_b, base, parity, [value[0:width, :]], [value[width : 2 * width, :]])


def route_y(extra, sc, *refs):
    count = 2 if extra else 1
    values, (xa, xb, ya, yb) = refs[:count], refs[count:]
    blank(extra, ya, yb)
    for value, (scale, base) in zip(values, layers(extra)):
        up, down = received(xa, xb, sc[0], scale, base)
        plus = [up(0, 32), down(0, 32), value[448 // scale : 608 // scale, :]]
        minus = [up(32, 64), down(32, 64), value[608 // scale : 768 // scale, :]]
        put_pair(ya, yb, base, sc[1], plus, minus)


def route_z(extra, sc, *refs):
    count = 2 if extra else 1
    values, (xa, xb, ya, yb, za, zb) = refs[:count], refs[count:]
    blank(extra, za, zb)
    for value, (scale, base) in zip(values, layers(extra)):
        x_up, x_down = received(xa, xb, sc[0], scale, base)
        y_up, y_down = received(ya, yb, sc[1], scale, base)
        both = []
        for x_at, y_at, own in ((64, (0, 32, 64), 768), (80, (8, 40, 80), 896)):
            pieces = [x_up(x_at, x_at + EDGE), x_down(x_at, x_at + EDGE)]
            for y in (y_up, y_down):
                for at, width in zip(y_at, (CORNER, CORNER, EDGE)):
                    pieces.append(y(at, at + width))
            pieces.append(value[own // scale : (own + FACE) // scale, :])
            both.append(pieces)
        put_pair(za, zb, base, sc[2], both[0], both[1])


def partner_pieces(sc, xa, xb, ya, yb, za, zb, scale, base):
    x_up, x_down = received(xa, xb, sc[0], scale, base)
    y_up, y_down = received(ya, yb, sc[1], scale, base)
    z_up, z_down = received(za, zb, sc[2], scale, base)
    pieces = []
    for (o1, o2, o3), _, width in SLOTS:
        s1, s2, s3 = -o1, -o2, -o3
        if s3:
            reader = z_up if s3 == 1 else z_down
            if s2:
                at = 32 if s2 == 1 else 64
                at += {1: 0, -1: CORNER, 0: 2 * CORNER}[s1]
            elif s1:
                at = 0 if s1 == 1 else EDGE
            else:
                at = 96
        elif s2:
            reader = y_up if s2 == 1 else y_down
            at = {1: EDGE, -1: 32 + EDGE, 0: 96}[s1]
        else:
            reader = x_up if s1 == 1 else x_down
            at = 96
        pieces.append(reader(at, at + width))
    return pieces


def pack_kernel(sc, order, load, modes, sel_ref, load_ref, comp_ref, mode, cols_ref, xa, xb, col, buf, mbuf, obuf, sems):
    copy_order = pltpu.make_async_copy(order, obuf, sems.at[2])
    copy_order.start()
    copy = pltpu.make_async_copy(load, buf, sems.at[0])
    copy.start()
    copy_modes = pltpu.make_async_copy(modes, mbuf, sems.at[1])
    copy_modes.start()
    copy_order.wait()
    turned = obuf[...].astype(F32).T.astype(jnp.int32)
    for offset, begin, width in SLOTS:
        lane, row = begin // 128, begin % 128
        col[OURS[offset] : OURS[offset] + width, :] = turned[row : row + width, lane : lane + 1]
    step = 256
    for at in range(0, ROWS, step):
        lanes = iota((step, ROWS), 1)
        sel_ref[at : at + step, :] = jnp.where(col[at : at + step, :] == lanes, 1.0, 0.0).astype(BF16)
    copy_modes.wait()
    top = jnp.concatenate([mbuf[...].astype(F32), jnp.zeros((16 - NMODE, ROWS), F32)], axis=0)
    mode[...] = top.astype(BF16)
    sel = sel_ref[...]
    copy.wait()
    both = dot(sel, jnp.concatenate([buf[...], top.T.astype(BF16)], axis=1))
    load_ref[...] = both[:, 0:128]
    cols = both[:, 128:].astype(BF16)
    cols_ref[...] = cols
    spread = jnp.where(iota((16, 128), 0) == iota((16, 128), 1) % 16, 1.0, 0.0).astype(BF16)
    wide = dot(cols, spread)
    keep = iota((ROWS, 128), 0) % GROUP == iota((ROWS, 128), 1) // 16
    wide = jnp.where(keep, wide, 0.0).astype(BF16)
    fold = jnp.where(iota((ROWS // GROUP, ROWS), 0) == iota((ROWS // GROUP, ROWS), 1) // GROUP, 1.0, 0.0)
    comp_ref[...] = dot(fold.astype(BF16), wide)
    send_x(sc[0], (load_ref, comp_ref), xa, xb, True)


def permute_kernel(sel, mode, order_row, dual, out, inv_ref, bt_ref, buf, sem):
    copy = pltpu.make_async_copy(dual, buf, sem)
    copy.start()
    packed = jnp.concatenate([order_row[:, begin : begin + width] for _, begin, width in SLOTS], axis=1)
    step = 256
    for at in range(0, ROWS, step):
        subs = iota((step, ROWS), 0) + at
        inv_ref[at : at + step, :] = jnp.where(packed == subs, 1.0, 0.0).astype(BF16)
    bt_ref[...] = dot(mode[...], inv_ref[...]).astype(BF16)
    copy.wait()
    for at in range(0, out.shape[0], step):
        rows = dot(sel[at : at + step, :], buf[...]).astype(BF16)
        out[at : at + step, :] = dot(rows, inv_ref[...]).astype(BF16)


def permute_rest_kernel(first, sel, inv, dual, inverse, out, near_inverse, sem):
    copy = pltpu.make_async_copy(inverse, near_inverse, sem)
    copy.start()
    step = 256
    for at in range(0, out.shape[0], step):
        rows = dot(sel[first + at : first + at + step, :], dual[...]).astype(BF16)
        out[at : at + step, :] = dot(rows, inv[...]).astype(BF16)
    copy.wait()


def project(sc, bt, residual, out):
    block = dot_wide(bt[...], residual)[0:8, :]
    count = sc[4].astype(F32)
    block = jnp.where(iota((8, 128), 0) == NMODE, count, block)
    for t in range(out.shape[0]):
        out[t, :, :] = block


def first_kernel(sc, load, bt, xa, xb, ya, yb, za, zb, res_ref, comp_ref, out):
    pieces = partner_pieces(sc, xa, xb, ya, yb, za, zb, 1, 0)
    at = 0
    for piece in pieces:
        end = at + piece.shape[0]
        res_ref[at:end, :] = load[at:end, :] + piece
        at = end
    project(sc, bt, res_ref[...], out)
    put(comp_ref, 0, partner_pieces(sc, xa, xb, ya, yb, za, zb, GROUP, BUNDLE))


def next_residual(sc, res, val, bundles, out):
    at = 0
    for piece in partner_pieces(sc, *bundles, 1, 0):
        end = at + piece.shape[0]
        out[at:end, :] = res[at:end, :] - (val[at:end, :] + piece)
        at = end


def step_kernel(sc, res, val, bt, xa, xb, ya, yb, za, zb, res_ref, out):
    next_residual(sc, res, val, (xa, xb, ya, yb, za, zb), res_ref)
    project(sc, bt, res_ref[...], out)


def last_kernel(sc, res, val, inv, xa, xb, ya, yb, za, zb, out, scratch):
    next_residual(sc, res, val, (xa, xb, ya, yb, za, zb), scratch)
    out[...] = dot_wide(inv[...], scratch[...])


def unpack_kernel(sc, inv, val, out):
    out[...] = dot_wide(inv[...], val[...])


def mode_kernel(sc, cols, comp, block, out):
    pick = jnp.where(iota((ROWS, 128), 0) // GROUP == iota((ROWS, 128), 1), 1.0, 0.0).astype(BF16)
    wide = dot(pick, comp[...].astype(BF16))
    keep = iota((ROWS, 128), 0) % GROUP == iota((ROWS, 128), 1) // 16
    wide = jnp.where(keep, wide, 0.0).astype(BF16)
    mode = iota((128, STACK), 0) % 16
    fold = jnp.where(mode == iota((128, STACK), 1) % NMODE, 1.0, 0.0).astype(BF16)
    theirs = dot(wide, fold)
    mode = iota((16, STACK), 0)
    own = jnp.where(mode == iota((16, STACK), 1) % NMODE, 1.0, 0.0).astype(BF16)
    mine = dot(cols[...], own)
    x_even, y_even = sc[0] == 0, sc[1] == 0
    which = jnp.where(
        x_even,
        jnp.where(y_even, block[:, 0:1], block[:, 1:2]),
        jnp.where(y_even, block[:, 2:3], block[:, 3:4]),
    )
    which = which + sc[2]
    at = iota((ROWS, STACK), 1) // NMODE
    home = 16 * sc[0] + 4 * sc[1] + 1 + sc[2]
    out[...] = (jnp.where(at == which, theirs, 0.0) + jnp.where(at == home, mine, 0.0)).astype(BF16)


def line_kernel(sc, line, inverse, mat_ref, out):
    everyone = line[...]
    size, coarse = everyone.shape[0], inverse.shape[0]
    counts = jnp.where(iota((size, 128), 0) % 8 == NMODE, everyone, 0.0).astype(BF16)

    def selection(rows, unit, first):
        position = iota((rows, size), 0) // unit + first
        col = iota((rows, size), 1)
        is_count = col % 8 == NMODE
        here = jnp.where(is_count & (col // 8 == position), 1.0, 0.0)
        before = jnp.where(is_count & (col // 8 < position), 1.0, 0.0)
        count = dot(here.astype(BF16), counts)
        offset = dot(before.astype(BF16), counts)
        mode = (iota((rows, 128), 0) % unit).astype(F32)
        compact = iota((rows, 128), 1).astype(F32)
        hit = (compact == offset + mode) & (mode < count)
        return jnp.where(hit, 1.0, 0.0)[:, 0:coarse]

    everywhere = selection(size, 8, 0)
    near = selection(NEAR, NMODE, sc[3] - sc[2] - 1)
    rows = jnp.dot(near, inverse[...], precision=HIGHEST, preferred_element_type=F32)
    matrix = lax.dot_general(rows, everywhere, (((1,), (1,)), ((), ())), precision=HIGHEST, preferred_element_type=F32)
    mat_ref[...] = matrix
    out[...] = jnp.dot(matrix, everyone, precision=HIGHEST, preferred_element_type=F32)


def solve_kernel(sc, line, matrix, out):
    out[...] = jnp.dot(matrix[...], line[...], precision=HIGHEST, preferred_element_type=F32)


def advance_kernel(keep, take, sc, *refs):
    if keep:
        res, modes, dual_a, dual_b, stack, old_dir, old_mul, dir_ref, mul_ref, val_ref, sa, sb = refs
    else:
        res, modes, dual_a, dual_b, stack, dir_ref, val_ref, sa, sb = refs
    corrected = res[...] - dot_wide(modes[...], stack[...])
    if keep:
        direction = keep * old_dir[...] + take * corrected
        mul_ref[...] = old_mul[...] + direction
    else:
        direction = corrected / take
    dir_ref[...] = direction
    rounded = direction.astype(BF16)
    val_ref[0 : ROWS // 2, :] = dot(dual_a[...], rounded)
    val_ref[ROWS // 2 :, :] = dot(dual_b[...], rounded)
    send_x(sc[0], (val_ref,), sa, sb, False)


def share(block, axis):
    size, line = lax.axis_size(axis), lax.axis_size("gz")
    groups = []
    for z in range(line):
        for even in range(0, size, 2):
            odd = (even + 1 if z % 2 == 0 else even - 1) % size
            groups.append([even * line + z, odd * line + z])
    block = lax.all_gather(block, (axis, "gz"), axis_index_groups=groups, tiled=True)
    return lax.all_gather(block, "gz", axis_index_groups=[[z, z + 1] for z in range(0, line, 2)], tiled=True)


def label(sign, odd):
    if sign == 0:
        return odd
    if odd:
        return 2 if sign == 1 else 0
    return 1 if sign == 1 else 3


def amplitude_blocks():
    out = np.zeros((ROWS, 4), np.int32)
    for x_odd in (0, 1):
        for y_odd in (0, 1):
            for (o1, o2, o3), _, width in SLOTS:
                at = OURS[(o1, o2, o3)]
                block = 4 * (4 * label(o1, x_odd) + label(o2, y_odd)) + o3 + 1
                out[at : at + width, 2 * x_odd + y_odd] = block
    return out


def cross(sc, value, x):
    pair = [((BUNDLE, 128), F32)] * 2
    y = exchange(*call(functools.partial(route_y, False), pair, sc, value, *x, name="route_y"), "gy")
    z = exchange(*call(functools.partial(route_z, False), pair, sc, value, *x, *y, name="route_z"), "gz")
    return (*x, *y, *z)


def local(dual_blocks, load_terms, row_order, mode_rows, mode_count, coarse_inverse):
    line_length = lax.axis_size("gz")
    pos = [lax.axis_index(axis) for axis in ("gx", "gy", "gz")]
    sc = jnp.stack([p % 2 for p in pos] + [pos[2], mode_count[0, 0, 0]]).astype(jnp.int32)
    inverse = in_hbm(coarse_inverse[0, 0])
    bundle = [((BUNDLE, 128), F32)] * 2
    vector = ((ROWS, 128), F32)
    square = ((ROWS, ROWS), BF16)
    wide = [((bundle_rows(True), 128), F32)] * 2
    gathered = ((line_length, 8, 128), F32)

    sel, load_rows, comp, mode, cols, sa, sb = pl.pallas_call(
        pack_kernel,
        out_shape=[
            jax.ShapeDtypeStruct(*v)
            for v in (
                square,
                vector,
                ((ROWS // GROUP, 128), F32),
                ((16, ROWS), BF16),
                ((ROWS, 16), BF16),
                *wide,
            )
        ],
        in_specs=[SMEM, HBM, HBM, HBM],
        out_specs=[VMEM] * 7,
        scratch_shapes=[
            pltpu.VMEM((ROWS, 1), jnp.int32),
            pltpu.VMEM((ROWS, 128), BF16),
            pltpu.VMEM((NMODE, ROWS), BF16),
            pltpu.VMEM((ROWS // 128, 128), jnp.int32),
            pltpu.SemaphoreType.DMA((3,)),
        ],
        compiler_params=pltpu.CompilerParams(vmem_limit_bytes=16 * 2**20),
        name="pack",
    )(sc, in_hbm(row_order[0, 0, 0].reshape(ROWS // 128, 128)), in_hbm(load_terms[0, 0, 0]), in_hbm(mode_rows[0, 0, 0].T))
    half = ((ROWS // 2, ROWS), BF16)
    x = exchange_async(sa, sb, "gx")
    dual_a, inv, bt = pl.pallas_call(
        permute_kernel,
        out_shape=[jax.ShapeDtypeStruct(*v) for v in (half, square, ((16, ROWS), BF16))],
        in_specs=[VMEM, VMEM, VMEM, HBM],
        out_specs=[VMEM] * 3,
        scratch_shapes=[pltpu.VMEM((ROWS, ROWS), BF16), pltpu.SemaphoreType.DMA],
        compiler_params=pltpu.CompilerParams(vmem_limit_bytes=16 * 2**20),
        name="permute",
    )(sel, mode, row_order[0, 0, 0][None, :], in_hbm(dual_blocks[0, 0, 0]))
    *x, dual_a, inv, bt = lax.optimization_barrier((*x, dual_a, inv, bt))
    values = (load_rows, comp)
    y = exchange_async(*call(functools.partial(route_y, True), wide, sc, *values, *x, name="route_y"), "gy")
    dual_b, near_inverse = pl.pallas_call(
        functools.partial(permute_rest_kernel, ROWS // 2),
        out_shape=[jax.ShapeDtypeStruct(*half), jax.ShapeDtypeStruct(inverse.shape, F32)],
        in_specs=[VMEM] * 3 + [HBM],
        out_specs=[VMEM] * 2,
        scratch_shapes=[pltpu.SemaphoreType.DMA],
        compiler_params=pltpu.CompilerParams(vmem_limit_bytes=12 * 2**20),
        name="permute_rest",
    )(sel, inv, dual_blocks[0, 0, 0], inverse)
    *y, dual_b, near_inverse = lax.optimization_barrier((*y, dual_b, near_inverse))
    z = exchange(*call(functools.partial(route_z, True), wide, sc, *values, *x, *y, name="route_z"), "gz")
    received_rows = (*x, *y, *z)
    residual, their_comp, proj = call(
        first_kernel,
        [vector, ((ROWS // GROUP, 128), F32), gathered],
        sc,
        load_rows,
        bt,
        *received_rows,
        name="first",
    )
    center_value = 0.5 * (EIG_HIGH + EIG_LOW)
    half_width = 0.5 * (EIG_HIGH - EIG_LOW)
    rho_prev = half_width / center_value
    amp = ((NEAR, 128), F32)
    for iteration in range(ITERS):
        line = lax.all_to_all(proj, "gz", 0, 0, tiled=True).reshape(8 * line_length, 128)
        if iteration == 0:
            near_matrix = ((NEAR, 8 * line_length), F32)
            matrix, own = call(line_kernel, [near_matrix, amp], sc, line, near_inverse, name="line")
            their_comp, own = lax.optimization_barrier((their_comp, own))
            (modes_near,) = call(
                mode_kernel, [((ROWS, STACK), BF16)], sc, cols, their_comp, jnp.asarray(amplitude_blocks()), name="modes"
            )
        else:
            (own,) = call(solve_kernel, [amp], sc, line, matrix, name="solve")
        near = (modes_near, dual_a, dual_b, share(share(own, "gy"), "gx"))
        if iteration == 0:
            direction, value, sa, sb = call(
                functools.partial(advance_kernel, None, center_value),
                [vector, vector, *bundle],
                sc,
                residual,
                *near,
                name="advance0",
            )
            multipliers = direction
        else:
            rho_now = 1.0 / (2.0 * center_value / half_width - rho_prev)
            direction, multipliers, value, sa, sb = call(
                functools.partial(advance_kernel, rho_now * rho_prev, 2.0 * rho_now / half_width),
                [vector, vector, vector, *bundle],
                sc,
                residual,
                *near,
                direction,
                multipliers,
                name="advance",
            )
            rho_prev = rho_now
        if iteration < ITERS - 1:
            received_rows = cross(sc, value, exchange(sa, sb, "gx"))
            residual, proj = call(
                step_kernel, [vector, gathered], sc, residual, value, bt, *received_rows, name="step"
            )
    x = exchange_async(sa, sb, "gx")
    (out_mul,) = call(unpack_kernel, [vector], sc, inv, multipliers, name="unpack")
    *x, out_mul = lax.optimization_barrier((*x, out_mul))
    received_rows = cross(sc, value, x)
    (out_res,) = call(
        last_kernel,
        [vector],
        sc,
        residual,
        value,
        inv,
        *received_rows,
        scratch=[pltpu.VMEM((ROWS, 128), F32)],
        name="last",
    )
    return out_mul[None, None, None], out_res[None, None, None]


def solution(mesh):
    in_specs = (
        P("gx", "gy", "gz", None, None),
        P("gx", "gy", "gz", None, None),
        P("gx", "gy", "gz", None),
        P("gx", "gy", "gz", None, None),
        P("gx", "gy", "gz"),
        P("gx", "gy", None, None),
    )
    out_specs = (P("gx", "gy", "gz", None, None), P("gx", "gy", "gz", None, None))
    return jax.shard_map(local, mesh=mesh, in_specs=in_specs, out_specs=out_specs, check_vma=False)
```

```python
import functools

import jax
import jax.numpy as jnp
import numpy as np
from jax import lax
from jax.experimental import pallas as pl
from jax.experimental.pallas import tpu as pltpu
from jax.sharding import PartitionSpec as P

FACE = 128
EDGE = 16
CORNER = 8
NMODE = 6
ITERS = 3
EIG_LOW = 0.5
EIG_HIGH = 6.0

F32 = jnp.float32
BF16 = jnp.bfloat16
HIGHEST = lax.Precision.HIGHEST
SIGNS = (1, -1, 0)
WIDTHS = {1: FACE, 2: EDGE, 3: CORNER}

BUNDLE = 224
NEAR = 4 * NMODE
STACK = 16 * NEAR
GROUP = 8


def tables():
    begin, row = {}, 0
    for weight in (1, 2, 3):
        for o1 in (-1, 0, 1):
            for o2 in (-1, 0, 1):
                for o3 in (-1, 0, 1):
                    if abs(o1) + abs(o2) + abs(o3) == weight:
                        begin[(o1, o2, o3)] = row
                        row += WIDTHS[weight]
    slots, ours, row = [], {}, 0
    for o1 in SIGNS:
        for o2 in SIGNS:
            for o3 in SIGNS:
                offset = (o1, o2, o3)
                if any(offset):
                    width = WIDTHS[abs(o1) + abs(o2) + abs(o3)]
                    slots.append((offset, begin[offset], width))
                    ours[offset] = row
                    row += width
    return slots, ours, row


SLOTS, OURS, ROWS = tables()


def swaps(size, parity):
    pairs = [(i, i + 1) for i in range(parity, size - 1, 2)]
    return pairs + [(j, i) for i, j in pairs]


def exchange(first, second, axis):
    size = lax.axis_size(axis)
    groups = [[i, i + 1] for i in range(0, size, 2)]
    other = lax.ppermute(second, axis, swaps(size, 1))
    return lax.all_gather(first, axis, axis_index_groups=groups, tiled=True), other


def exchange_async(first, second, axis):
    size = lax.axis_size(axis)
    return lax.ppermute(first, axis, swaps(size, 0)), lax.ppermute(second, axis, swaps(size, 1))


VMEM = pl.BlockSpec(memory_space=pltpu.VMEM)
HBM = pl.BlockSpec(memory_space=pltpu.HBM)
SMEM = pl.BlockSpec(memory_space=pltpu.SMEM)


def call(kernel, out_shape, scalars, *args, scratch=(), name=None, limit=12):
    return pl.pallas_call(
        kernel,
        out_shape=[jax.ShapeDtypeStruct(s, t) for s, t in out_shape],
        in_specs=[SMEM] + [VMEM] * len(args),
        out_specs=[VMEM] * len(out_shape),
        scratch_shapes=list(scratch),
        compiler_params=pltpu.CompilerParams(vmem_limit_bytes=limit * 2**20),
        name=name,
    )(scalars, *args)


def in_hbm(x):
    return pltpu.with_memory_space_constraint(x, pltpu.HBM)


def dot(a, b):
    return jnp.dot(a, b, preferred_element_type=F32)


def dot_t(a, b):
    return lax.dot_general(a, b, (((1,), (1,)), ((), ())), preferred_element_type=F32)


def dot_wide(a, x):
    high = x.astype(BF16)
    low = (x - high.astype(F32)).astype(BF16)
    out = dot(a, jnp.concatenate([high, low], axis=1))
    width = x.shape[1]
    return out[:, 0:width] + out[:, width:]


def iota(shape, dim):
    return lax.broadcasted_iota(jnp.int32, shape, dim)


def layers(extra):
    return [(1, 0), (GROUP, BUNDLE)] if extra else [(1, 0)]


def bundle_rows(extra):
    return BUNDLE + 32 if extra else BUNDLE


def put(ref, at, pieces):
    for piece in pieces:
        ref[at : at + piece.shape[0], :] = piece
        at += piece.shape[0]


def put_pair(ref_a, ref_b, at, parity, plus, minus):
    even = parity == 0
    put(ref_a, at, [jnp.where(even, p, m) for p, m in zip(plus, minus)])
    put(ref_b, at, [jnp.where(even, m, p) for p, m in zip(plus, minus)])


def received(ref_a, ref_b, parity, scale, base):
    even = parity == 0
    rows = ref_b.shape[0]
    paired = ref_a.shape[0] > rows

    def cut(ref, a, b, shift=0):
        return ref[shift + base + a // scale : shift + base + b // scale, :]

    def up(a, b):
        return jnp.where(even, cut(ref_b, a, b), cut(ref_a, a, b))

    def down(a, b):
        return jnp.where(even, cut(ref_a, a, b, rows if paired else 0), cut(ref_b, a, b))

    return up, down


def blank(extra, *refs):
    if extra:
        for ref in refs:
            ref[bundle_rows(extra) - 8 :, :] = jnp.zeros((8, 128), F32)


def send_x(parity, values, send_a, send_b, extra):
    blank(extra, send_a, send_b)
    for value, (scale, base) in zip(values, layers(extra)):
        width = BUNDLE // scale
        put_pair(send_a, send_b, base, parity, [value[0:width, :]], [value[width : 2 * width, :]])


def route_y(extra, sc, *refs):
    count = 2 if extra else 1
    values, (xa, xb, ya, yb) = refs[:count], refs[count:]
    blank(extra, ya, yb)
    for value, (scale, base) in zip(values, layers(extra)):
        up, down = received(xa, xb, sc[0], scale, base)
        plus = [up(0, 32), down(0, 32), value[448 // scale : 608 // scale, :]]
        minus = [up(32, 64), down(32, 64), value[608 // scale : 768 // scale, :]]
        put_pair(ya, yb, base, sc[1], plus, minus)


def route_z(extra, sc, *refs):
    count = 2 if extra else 1
    values, (xa, xb, ya, yb, za, zb) = refs[:count], refs[count:]
    blank(extra, za, zb)
    for value, (scale, base) in zip(values, layers(extra)):
        x_up, x_down = received(xa, xb, sc[0], scale, base)
        y_up, y_down = received(ya, yb, sc[1], scale, base)
        both = []
        for x_at, y_at, own in ((64, (0, 32, 64), 768), (80, (8, 40, 80), 896)):
            pieces = [x_up(x_at, x_at + EDGE), x_down(x_at, x_at + EDGE)]
            for y in (y_up, y_down):
                for at, width in zip(y_at, (CORNER, CORNER, EDGE)):
                    pieces.append(y(at, at + width))
            pieces.append(value[own // scale : (own + FACE) // scale, :])
            both.append(pieces)
        put_pair(za, zb, base, sc[2], both[0], both[1])


def partner_pieces(sc, xa, xb, ya, yb, za, zb, scale, base):
    x_up, x_down = received(xa, xb, sc[0], scale, base)
    y_up, y_down = received(ya, yb, sc[1], scale, base)
    z_up, z_down = received(za, zb, sc[2], scale, base)
    pieces = []
    for (o1, o2, o3), _, width in SLOTS:
        s1, s2, s3 = -o1, -o2, -o3
        if s3:
            reader = z_up if s3 == 1 else z_down
            if s2:
                at = 32 if s2 == 1 else 64
                at += {1: 0, -1: CORNER, 0: 2 * CORNER}[s1]
            elif s1:
                at = 0 if s1 == 1 else EDGE
            else:
                at = 96
        elif s2:
            reader = y_up if s2 == 1 else y_down
            at = {1: EDGE, -1: 32 + EDGE, 0: 96}[s1]
        else:
            reader = x_up if s1 == 1 else x_down
            at = 96
        pieces.append(reader(at, at + width))
    return pieces


def pack_kernel(sc, order, load, modes, sel_ref, load_ref, comp_ref, mode, cols_ref, order_ref, xa, xb, col, buf, mbuf, sems):
    copy_order = pltpu.make_async_copy(order, order_ref, sems.at[2])
    copy_order.start()
    copy = pltpu.make_async_copy(load, buf, sems.at[0])
    copy.start()
    copy_modes = pltpu.make_async_copy(modes, mbuf, sems.at[1])
    copy_modes.start()
    copy_order.wait()
    turned = order_ref[...].astype(F32).T.astype(jnp.int32)
    for offset, begin, width in SLOTS:
        lane, row = begin // 128, begin % 128
        col[OURS[offset] : OURS[offset] + width, :] = turned[row : row + width, lane : lane + 1]
    step = 256
    for at in range(0, ROWS, step):
        lanes = iota((step, ROWS), 1)
        sel_ref[at : at + step, :] = jnp.where(col[at : at + step, :] == lanes, 1.0, 0.0).astype(BF16)
    copy_modes.wait()
    top = jnp.concatenate([mbuf[...].astype(F32), jnp.zeros((16 - NMODE, ROWS), F32)], axis=0)
    mode[...] = top.astype(BF16)
    sel = sel_ref[...]
    copy.wait()
    both = dot(sel, jnp.concatenate([buf[...], top.T.astype(BF16)], axis=1))
    load_ref[...] = both[:, 0:128]
    cols = both[:, 128:].astype(BF16)
    cols_ref[...] = cols
    spread = jnp.where(iota((16, 128), 0) == iota((16, 128), 1) % 16, 1.0, 0.0).astype(BF16)
    wide = dot(cols, spread)
    keep = iota((ROWS, 128), 0) % GROUP == iota((ROWS, 128), 1) // 16
    wide = jnp.where(keep, wide, 0.0).astype(BF16)
    fold = jnp.where(iota((ROWS // GROUP, ROWS), 0) == iota((ROWS // GROUP, ROWS), 1) // GROUP, 1.0, 0.0)
    comp_ref[...] = dot(fold.astype(BF16), wide)
    send_x(sc[0], (load_ref, comp_ref), xa, xb, True)


def permute_kernel(sel, mode, order, dual, out, inv_ref, bt_ref, buf, sem):
    copy = pltpu.make_async_copy(dual, buf, sem)
    copy.start()
    pieces = []
    for _, begin, width in SLOTS:
        row, lane = begin // 128, begin % 128
        pieces.append(order[row : row + 1, lane : lane + width])
    packed = jnp.concatenate(pieces, axis=1)
    step = 256
    for at in range(0, ROWS, step):
        subs = iota((step, ROWS), 0) + at
        inv_ref[at : at + step, :] = jnp.where(packed == subs, 1.0, 0.0).astype(BF16)
    bt_ref[...] = dot(mode[...], inv_ref[...]).astype(BF16)
    copy.wait()
    for at in range(0, out.shape[0], step):
        rows = dot(sel[at : at + step, :], buf[...]).astype(BF16)
        out[at : at + step, :] = dot(rows, inv_ref[...]).astype(BF16)


def permute_rest_kernel(first, sel, inv, dual, inverse, out, near_inverse, sem):
    copy = pltpu.make_async_copy(inverse, near_inverse, sem)
    copy.start()
    step = 256
    for at in range(0, out.shape[0], step):
        rows = dot(sel[first + at : first + at + step, :], dual[...]).astype(BF16)
        out[at : at + step, :] = dot(rows, inv[...]).astype(BF16)
    copy.wait()


def project(sc, bt, residual, out):
    block = dot_wide(bt[...], residual)[0:8, :]
    count = sc[4].astype(F32)
    block = jnp.where(iota((8, 128), 0) == NMODE, count, block)
    for t in range(out.shape[0]):
        out[t, :, :] = block


def first_kernel(sc, load, bt, xa, xb, ya, yb, za, zb, res_ref, comp_ref, out):
    pieces = partner_pieces(sc, xa, xb, ya, yb, za, zb, 1, 0)
    at = 0
    for piece in pieces:
        end = at + piece.shape[0]
        res_ref[at:end, :] = load[at:end, :] + piece
        at = end
    project(sc, bt, res_ref[...], out)
    put(comp_ref, 0, partner_pieces(sc, xa, xb, ya, yb, za, zb, GROUP, BUNDLE))


def next_residual(sc, res, val, bundles, out):
    at = 0
    for piece in partner_pieces(sc, *bundles, 1, 0):
        end = at + piece.shape[0]
        out[at:end, :] = res[at:end, :] - (val[at:end, :] + piece)
        at = end


def step_kernel(sc, res, val, bt, xa, xb, ya, yb, za, zb, res_ref, out):
    next_residual(sc, res, val, (xa, xb, ya, yb, za, zb), res_ref)
    project(sc, bt, res_ref[...], out)


def last_kernel(sc, res, val, inv, xa, xb, ya, yb, za, zb, out, scratch):
    next_residual(sc, res, val, (xa, xb, ya, yb, za, zb), scratch)
    out[...] = dot_wide(inv[...], scratch[...])


def unpack_kernel(sc, inv, val, out):
    out[...] = dot_wide(inv[...], val[...])


def mode_kernel(sc, cols, comp, block, out):
    pick = jnp.where(iota((ROWS, 128), 0) // GROUP == iota((ROWS, 128), 1), 1.0, 0.0).astype(BF16)
    wide = dot(pick, comp[...].astype(BF16))
    keep = iota((ROWS, 128), 0) % GROUP == iota((ROWS, 128), 1) // 16
    wide = jnp.where(keep, wide, 0.0).astype(BF16)
    mode = iota((128, STACK), 0) % 16
    fold = jnp.where(mode == iota((128, STACK), 1) % NMODE, 1.0, 0.0).astype(BF16)
    theirs = dot(wide, fold)
    mode = iota((16, STACK), 0)
    own = jnp.where(mode == iota((16, STACK), 1) % NMODE, 1.0, 0.0).astype(BF16)
    mine = dot(cols[...], own)
    x_even, y_even = sc[0] == 0, sc[1] == 0
    which = jnp.where(
        x_even,
        jnp.where(y_even, block[:, 0:1], block[:, 1:2]),
        jnp.where(y_even, block[:, 2:3], block[:, 3:4]),
    )
    which = which + sc[2]
    at = iota((ROWS, STACK), 1) // NMODE
    home = 16 * sc[0] + 4 * sc[1] + 1 + sc[2]
    out[...] = (jnp.where(at == which, theirs, 0.0) + jnp.where(at == home, mine, 0.0)).astype(BF16)


def line_kernel(sc, line, inverse, mat_ref, out):
    everyone = line[...]
    size, coarse = everyone.shape[0], inverse.shape[0]
    counts = jnp.where(iota((size, 128), 0) % 8 == NMODE, everyone, 0.0).astype(BF16)

    def selection(rows, unit, first):
        position = iota((rows, size), 0) // unit + first
        col = iota((rows, size), 1)
        is_count = col % 8 == NMODE
        here = jnp.where(is_count & (col // 8 == position), 1.0, 0.0)
        before = jnp.where(is_count & (col // 8 < position), 1.0, 0.0)
        count = dot(here.astype(BF16), counts)
        offset = dot(before.astype(BF16), counts)
        mode = (iota((rows, 128), 0) % unit).astype(F32)
        compact = iota((rows, 128), 1).astype(F32)
        hit = (compact == offset + mode) & (mode < count)
        return jnp.where(hit, 1.0, 0.0)[:, 0:coarse]

    everywhere = selection(size, 8, 0)
    near = selection(NEAR, NMODE, sc[3] - sc[2] - 1)
    rows = jnp.dot(near, inverse[...], precision=HIGHEST, preferred_element_type=F32)
    matrix = lax.dot_general(rows, everywhere, (((1,), (1,)), ((), ())), precision=HIGHEST, preferred_element_type=F32)
    mat_ref[...] = matrix
    out[...] = jnp.dot(matrix, everyone, precision=HIGHEST, preferred_element_type=F32)


def solve_kernel(sc, line, matrix, out):
    out[...] = jnp.dot(matrix[...], line[...], precision=HIGHEST, preferred_element_type=F32)


def advance_kernel(keep, take, sc, *refs):
    if keep:
        res, modes, dual_a, dual_b, stack, old_dir, old_mul, dir_ref, mul_ref, val_ref, sa, sb = refs
    else:
        res, modes, dual_a, dual_b, stack, dir_ref, val_ref, sa, sb = refs
    corrected = res[...] - dot_wide(modes[...], stack[...])
    if keep:
        direction = keep * old_dir[...] + take * corrected
        mul_ref[...] = old_mul[...] + direction
    else:
        direction = corrected / take
    dir_ref[...] = direction
    rounded = direction.astype(BF16)
    val_ref[0 : ROWS // 2, :] = dot(dual_a[...], rounded)
    val_ref[ROWS // 2 :, :] = dot(dual_b[...], rounded)
    send_x(sc[0], (val_ref,), sa, sb, False)


def share(block, axis):
    size, line = lax.axis_size(axis), lax.axis_size("gz")
    groups = []
    for z in range(line):
        for even in range(0, size, 2):
            odd = (even + 1 if z % 2 == 0 else even - 1) % size
            groups.append([even * line + z, odd * line + z])
    block = lax.all_gather(block, (axis, "gz"), axis_index_groups=groups, tiled=True)
    return lax.all_gather(block, "gz", axis_index_groups=[[z, z + 1] for z in range(0, line, 2)], tiled=True)


def label(sign, odd):
    if sign == 0:
        return odd
    if odd:
        return 2 if sign == 1 else 0
    return 1 if sign == 1 else 3


def amplitude_blocks():
    out = np.zeros((ROWS, 4), np.int32)
    for x_odd in (0, 1):
        for y_odd in (0, 1):
            for (o1, o2, o3), _, width in SLOTS:
                at = OURS[(o1, o2, o3)]
                block = 4 * (4 * label(o1, x_odd) + label(o2, y_odd)) + o3 + 1
                out[at : at + width, 2 * x_odd + y_odd] = block
    return out


def cross(sc, value, x):
    pair = [((BUNDLE, 128), F32)] * 2
    y = exchange(*call(functools.partial(route_y, False), pair, sc, value, *x, name="route_y"), "gy")
    z = exchange(*call(functools.partial(route_z, False), pair, sc, value, *x, *y, name="route_z"), "gz")
    return (*x, *y, *z)


def local(dual_blocks, load_terms, row_order, mode_rows, mode_count, coarse_inverse):
    line_length = lax.axis_size("gz")
    pos = [lax.axis_index(axis) for axis in ("gx", "gy", "gz")]
    sc = jnp.stack([p % 2 for p in pos] + [pos[2], mode_count[0, 0, 0]]).astype(jnp.int32)
    inverse = in_hbm(coarse_inverse[0, 0])
    bundle = [((BUNDLE, 128), F32)] * 2
    vector = ((ROWS, 128), F32)
    square = ((ROWS, ROWS), BF16)
    wide = [((bundle_rows(True), 128), F32)] * 2
    gathered = ((line_length, 8, 128), F32)

    sel, load_rows, comp, mode, cols, order, sa, sb = pl.pallas_call(
        pack_kernel,
        out_shape=[
            jax.ShapeDtypeStruct(*v)
            for v in (
                square,
                vector,
                ((ROWS // GROUP, 128), F32),
                ((16, ROWS), BF16),
                ((ROWS, 16), BF16),
                ((ROWS // 128, 128), jnp.int32),
                *wide,
            )
        ],
        in_specs=[SMEM, HBM, HBM, HBM],
        out_specs=[VMEM] * 8,
        scratch_shapes=[
            pltpu.VMEM((ROWS, 1), jnp.int32),
            pltpu.VMEM((ROWS, 128), BF16),
            pltpu.VMEM((NMODE, ROWS), BF16),
            pltpu.SemaphoreType.DMA((3,)),
        ],
        compiler_params=pltpu.CompilerParams(vmem_limit_bytes=16 * 2**20),
        name="pack",
    )(sc, in_hbm(row_order[0, 0, 0].reshape(ROWS // 128, 128)), in_hbm(load_terms[0, 0, 0]), in_hbm(mode_rows[0, 0, 0].T))
    half = ((ROWS // 2, ROWS), BF16)
    x = exchange_async(sa, sb, "gx")
    dual_a, inv, bt = pl.pallas_call(
        permute_kernel,
        out_shape=[jax.ShapeDtypeStruct(*v) for v in (half, square, ((16, ROWS), BF16))],
        in_specs=[VMEM, VMEM, VMEM, HBM],
        out_specs=[VMEM] * 3,
        scratch_shapes=[pltpu.VMEM((ROWS, ROWS), BF16), pltpu.SemaphoreType.DMA],
        compiler_params=pltpu.CompilerParams(vmem_limit_bytes=16 * 2**20),
        name="permute",
    )(sel, mode, order, in_hbm(dual_blocks[0, 0, 0]))
    *x, dual_a, inv, bt = lax.optimization_barrier((*x, dual_a, inv, bt))
    values = (load_rows, comp)
    y = exchange_async(*call(functools.partial(route_y, True), wide, sc, *values, *x, name="route_y"), "gy")
    dual_b, near_inverse = pl.pallas_call(
        functools.partial(permute_rest_kernel, ROWS // 2),
        out_shape=[jax.ShapeDtypeStruct(*half), jax.ShapeDtypeStruct(inverse.shape, F32)],
        in_specs=[VMEM] * 3 + [HBM],
        out_specs=[VMEM] * 2,
        scratch_shapes=[pltpu.SemaphoreType.DMA],
        compiler_params=pltpu.CompilerParams(vmem_limit_bytes=12 * 2**20),
        name="permute_rest",
    )(sel, inv, dual_blocks[0, 0, 0], inverse)
    *y, dual_b, near_inverse = lax.optimization_barrier((*y, dual_b, near_inverse))
    z = exchange(*call(functools.partial(route_z, True), wide, sc, *values, *x, *y, name="route_z"), "gz")
    received_rows = (*x, *y, *z)
    residual, their_comp, proj = call(
        first_kernel,
        [vector, ((ROWS // GROUP, 128), F32), gathered],
        sc,
        load_rows,
        bt,
        *received_rows,
        name="first",
    )
    center_value = 0.5 * (EIG_HIGH + EIG_LOW)
    half_width = 0.5 * (EIG_HIGH - EIG_LOW)
    rho_prev = half_width / center_value
    amp = ((NEAR, 128), F32)
    for iteration in range(ITERS):
        line = lax.all_to_all(proj, "gz", 0, 0, tiled=True).reshape(8 * line_length, 128)
        if iteration == 0:
            near_matrix = ((NEAR, 8 * line_length), F32)
            matrix, own = call(line_kernel, [near_matrix, amp], sc, line, near_inverse, name="line")
            their_comp, own = lax.optimization_barrier((their_comp, own))
            (modes_near,) = call(
                mode_kernel, [((ROWS, STACK), BF16)], sc, cols, their_comp, jnp.asarray(amplitude_blocks()), name="modes"
            )
        else:
            (own,) = call(solve_kernel, [amp], sc, line, matrix, name="solve")
        near = (modes_near, dual_a, dual_b, share(share(own, "gy"), "gx"))
        if iteration == 0:
            direction, value, sa, sb = call(
                functools.partial(advance_kernel, None, center_value),
                [vector, vector, *bundle],
                sc,
                residual,
                *near,
                name="advance0",
            )
            multipliers = direction
        else:
            rho_now = 1.0 / (2.0 * center_value / half_width - rho_prev)
            direction, multipliers, value, sa, sb = call(
                functools.partial(advance_kernel, rho_now * rho_prev, 2.0 * rho_now / half_width),
                [vector, vector, vector, *bundle],
                sc,
                residual,
                *near,
                direction,
                multipliers,
                name="advance",
            )
            rho_prev = rho_now
        if iteration < ITERS - 1:
            received_rows = cross(sc, value, exchange(sa, sb, "gx"))
            residual, proj = call(
                step_kernel, [vector, gathered], sc, residual, value, bt, *received_rows, name="step"
            )
    x = exchange_async(sa, sb, "gx")
    (out_mul,) = call(unpack_kernel, [vector], sc, inv, multipliers, name="unpack")
    *x, out_mul = lax.optimization_barrier((*x, out_mul))
    received_rows = cross(sc, value, x)
    (out_res,) = call(
        last_kernel,
        [vector],
        sc,
        residual,
        value,
        inv,
        *received_rows,
        scratch=[pltpu.VMEM((ROWS, 128), F32)],
        name="last",
    )
    return out_mul[None, None, None], out_res[None, None, None]


def solution(mesh):
    in_specs = (
        P("gx", "gy", "gz", None, None),
        P("gx", "gy", "gz", None, None),
        P("gx", "gy", "gz", None),
        P("gx", "gy", "gz", None, None),
        P("gx", "gy", "gz"),
        P("gx", "gy", None, None),
    )
    out_specs = (P("gx", "gy", "gz", None, None), P("gx", "gy", "gz", None, None))
    return jax.shard_map(local, mesh=mesh, in_specs=in_specs, out_specs=out_specs, check_vma=False)
```

```python
import functools

import jax
import jax.numpy as jnp
import numpy as np
from jax import lax
from jax.experimental import pallas as pl
from jax.experimental.pallas import tpu as pltpu
from jax.sharding import PartitionSpec as P

FACE = 128
EDGE = 16
CORNER = 8
NMODE = 6
ITERS = 3
EIG_LOW = 0.5
EIG_HIGH = 6.0

F32 = jnp.float32
BF16 = jnp.bfloat16
HIGHEST = lax.Precision.HIGHEST
SIGNS = (1, -1, 0)
WIDTHS = {1: FACE, 2: EDGE, 3: CORNER}

BUNDLE = 224
NEAR = 4 * NMODE
STACK = 16 * NEAR
GROUP = 8


def tables():
    begin, row = {}, 0
    for weight in (1, 2, 3):
        for o1 in (-1, 0, 1):
            for o2 in (-1, 0, 1):
                for o3 in (-1, 0, 1):
                    if abs(o1) + abs(o2) + abs(o3) == weight:
                        begin[(o1, o2, o3)] = row
                        row += WIDTHS[weight]
    slots, ours, row = [], {}, 0
    for o1 in SIGNS:
        for o2 in SIGNS:
            for o3 in SIGNS:
                offset = (o1, o2, o3)
                if any(offset):
                    width = WIDTHS[abs(o1) + abs(o2) + abs(o3)]
                    slots.append((offset, begin[offset], width))
                    ours[offset] = row
                    row += width
    return slots, ours, row


SLOTS, OURS, ROWS = tables()


def swaps(size, parity):
    pairs = [(i, i + 1) for i in range(parity, size - 1, 2)]
    return pairs + [(j, i) for i, j in pairs]


def exchange(first, second, axis):
    size = lax.axis_size(axis)
    groups = [[i, i + 1] for i in range(0, size, 2)]
    other = lax.ppermute(second, axis, swaps(size, 1))
    return lax.all_gather(first, axis, axis_index_groups=groups, tiled=True), other


def exchange_async(first, second, axis):
    size = lax.axis_size(axis)
    return lax.ppermute(first, axis, swaps(size, 0)), lax.ppermute(second, axis, swaps(size, 1))


VMEM = pl.BlockSpec(memory_space=pltpu.VMEM)
HBM = pl.BlockSpec(memory_space=pltpu.HBM)
SMEM = pl.BlockSpec(memory_space=pltpu.SMEM)


def call(kernel, out_shape, scalars, *args, scratch=(), name=None, limit=12):
    return pl.pallas_call(
        kernel,
        out_shape=[jax.ShapeDtypeStruct(s, t) for s, t in out_shape],
        in_specs=[SMEM] + [VMEM] * len(args),
        out_specs=[VMEM] * len(out_shape),
        scratch_shapes=list(scratch),
        compiler_params=pltpu.CompilerParams(vmem_limit_bytes=limit * 2**20),
        name=name,
    )(scalars, *args)


def in_hbm(x):
    return pltpu.with_memory_space_constraint(x, pltpu.HBM)


def dot(a, b):
    return jnp.dot(a, b, preferred_element_type=F32)


def dot_t(a, b):
    return lax.dot_general(a, b, (((1,), (1,)), ((), ())), preferred_element_type=F32)


def dot_wide(a, x):
    high = x.astype(BF16)
    low = (x - high.astype(F32)).astype(BF16)
    out = dot(a, jnp.concatenate([high, low], axis=1))
    width = x.shape[1]
    return out[:, 0:width] + out[:, width:]


def iota(shape, dim):
    return lax.broadcasted_iota(jnp.int32, shape, dim)


def layers(extra):
    return [(1, 0), (GROUP, BUNDLE)] if extra else [(1, 0)]


def bundle_rows(extra):
    return BUNDLE + 32 if extra else BUNDLE


def put(ref, at, pieces):
    for piece in pieces:
        ref[at : at + piece.shape[0], :] = piece
        at += piece.shape[0]


def put_pair(ref_a, ref_b, at, parity, plus, minus):
    even = parity == 0
    put(ref_a, at, [jnp.where(even, p, m) for p, m in zip(plus, minus)])
    put(ref_b, at, [jnp.where(even, m, p) for p, m in zip(plus, minus)])


def received(ref_a, ref_b, parity, scale, base):
    even = parity == 0
    rows = ref_b.shape[0]
    paired = ref_a.shape[0] > rows

    def cut(ref, a, b, shift=0):
        return ref[shift + base + a // scale : shift + base + b // scale, :]

    def up(a, b):
        return jnp.where(even, cut(ref_b, a, b), cut(ref_a, a, b))

    def down(a, b):
        return jnp.where(even, cut(ref_a, a, b, rows if paired else 0), cut(ref_b, a, b))

    return up, down


def blank(extra, *refs):
    if extra:
        for ref in refs:
            ref[bundle_rows(extra) - 8 :, :] = jnp.zeros((8, 128), F32)


def send_x(parity, values, send_a, send_b, extra):
    blank(extra, send_a, send_b)
    for value, (scale, base) in zip(values, layers(extra)):
        width = BUNDLE // scale
        put_pair(send_a, send_b, base, parity, [value[0:width, :]], [value[width : 2 * width, :]])


def route_y(extra, sc, *refs):
    count = 2 if extra else 1
    values, (xa, xb, ya, yb) = refs[:count], refs[count:]
    blank(extra, ya, yb)
    for value, (scale, base) in zip(values, layers(extra)):
        up, down = received(xa, xb, sc[0], scale, base)
        plus = [up(0, 32), down(0, 32), value[448 // scale : 608 // scale, :]]
        minus = [up(32, 64), down(32, 64), value[608 // scale : 768 // scale, :]]
        put_pair(ya, yb, base, sc[1], plus, minus)


def route_z(extra, sc, *refs):
    count = 2 if extra else 1
    values, (xa, xb, ya, yb, za, zb) = refs[:count], refs[count:]
    blank(extra, za, zb)
    for value, (scale, base) in zip(values, layers(extra)):
        x_up, x_down = received(xa, xb, sc[0], scale, base)
        y_up, y_down = received(ya, yb, sc[1], scale, base)
        both = []
        for x_at, y_at, own in ((64, (0, 32, 64), 768), (80, (8, 40, 80), 896)):
            pieces = [x_up(x_at, x_at + EDGE), x_down(x_at, x_at + EDGE)]
            for y in (y_up, y_down):
                for at, width in zip(y_at, (CORNER, CORNER, EDGE)):
                    pieces.append(y(at, at + width))
            pieces.append(value[own // scale : (own + FACE) // scale, :])
            both.append(pieces)
        put_pair(za, zb, base, sc[2], both[0], both[1])


def partner_pieces(sc, xa, xb, ya, yb, za, zb, scale, base):
    x_up, x_down = received(xa, xb, sc[0], scale, base)
    y_up, y_down = received(ya, yb, sc[1], scale, base)
    z_up, z_down = received(za, zb, sc[2], scale, base)
    pieces = []
    for (o1, o2, o3), _, width in SLOTS:
        s1, s2, s3 = -o1, -o2, -o3
        if s3:
            reader = z_up if s3 == 1 else z_down
            if s2:
                at = 32 if s2 == 1 else 64
                at += {1: 0, -1: CORNER, 0: 2 * CORNER}[s1]
            elif s1:
                at = 0 if s1 == 1 else EDGE
            else:
                at = 96
        elif s2:
            reader = y_up if s2 == 1 else y_down
            at = {1: EDGE, -1: 32 + EDGE, 0: 96}[s1]
        else:
            reader = x_up if s1 == 1 else x_down
            at = 96
        pieces.append(reader(at, at + width))
    return pieces


def pack_kernel(sc, order, load, modes, sel_ref, load_ref, comp_ref, mode, cols_ref, order_ref, xa, xb, col, buf, mbuf, sems):
    copy_order = pltpu.make_async_copy(order, order_ref, sems.at[2])
    copy_order.start()
    copy = pltpu.make_async_copy(load, buf, sems.at[0])
    copy.start()
    copy_modes = pltpu.make_async_copy(modes, mbuf, sems.at[1])
    copy_modes.start()
    copy_order.wait()
    turned = order_ref[...].astype(F32).T.astype(jnp.int32)
    for offset, begin, width in SLOTS:
        lane, row = begin // 128, begin % 128
        col[OURS[offset] : OURS[offset] + width, :] = turned[row : row + width, lane : lane + 1]
    step = 256
    for at in range(0, ROWS, step):
        lanes = iota((step, ROWS), 1)
        sel_ref[at : at + step, :] = jnp.where(col[at : at + step, :] == lanes, 1.0, 0.0).astype(BF16)
    copy_modes.wait()
    top = jnp.concatenate([mbuf[...].astype(F32), jnp.zeros((16 - NMODE, ROWS), F32)], axis=0)
    mode[...] = top.astype(BF16)
    sel = sel_ref[...]
    copy.wait()
    both = dot(sel, jnp.concatenate([buf[...], top.T.astype(BF16)], axis=1))
    load_ref[...] = both[:, 0:128]
    cols = both[:, 128:].astype(BF16)
    cols_ref[...] = cols
    spread = jnp.where(iota((16, 128), 0) == iota((16, 128), 1) % 16, 1.0, 0.0).astype(BF16)
    wide = dot(cols, spread)
    keep = iota((ROWS, 128), 0) % GROUP == iota((ROWS, 128), 1) // 16
    wide = jnp.where(keep, wide, 0.0).astype(BF16)
    fold = jnp.where(iota((ROWS // GROUP, ROWS), 0) == iota((ROWS // GROUP, ROWS), 1) // GROUP, 1.0, 0.0)
    comp_ref[...] = dot(fold.astype(BF16), wide)
    send_x(sc[0], (load_ref, comp_ref), xa, xb, True)


def permute_kernel(sel, mode, order, dual, out, inv_ref, bt_ref, buf, sem):
    copy = pltpu.make_async_copy(dual, buf, sem)
    copy.start()
    pieces = []
    for _, begin, width in SLOTS:
        row, lane = begin // 128, begin % 128
        pieces.append(order[row : row + 1, lane : lane + width])
    packed = jnp.concatenate(pieces, axis=1)
    step = 256
    for at in range(0, ROWS, step):
        subs = iota((step, ROWS), 0) + at
        inv_ref[at : at + step, :] = jnp.where(packed == subs, 1.0, 0.0).astype(BF16)
    bt_ref[...] = dot(mode[...], inv_ref[...]).astype(BF16)
    copy.wait()
    for at in range(0, out.shape[0], step):
        rows = dot(sel[at : at + step, :], buf[...]).astype(BF16)
        out[at : at + step, :] = dot(rows, inv_ref[...]).astype(BF16)


def permute_rest_kernel(first, sel, inv, dual, inverse, out, near_inverse, sem):
    copy = pltpu.make_async_copy(inverse, near_inverse, sem)
    copy.start()
    step = 256
    for at in range(0, out.shape[0], step):
        rows = dot(sel[first + at : first + at + step, :], dual[...]).astype(BF16)
        out[at : at + step, :] = dot(rows, inv[...]).astype(BF16)
    copy.wait()


def project(sc, bt, residual, out):
    block = dot_wide(bt[...], residual)[0:8, :]
    count = sc[4].astype(F32)
    block = jnp.where(iota((8, 128), 0) == NMODE, count, block)
    for t in range(out.shape[0]):
        out[t, :, :] = block


def first_kernel(sc, load, bt, xa, xb, ya, yb, za, zb, res_ref, comp_ref, out):
    pieces = partner_pieces(sc, xa, xb, ya, yb, za, zb, 1, 0)
    at = 0
    for piece in pieces:
        end = at + piece.shape[0]
        res_ref[at:end, :] = load[at:end, :] + piece
        at = end
    project(sc, bt, res_ref[...], out)
    put(comp_ref, 0, partner_pieces(sc, xa, xb, ya, yb, za, zb, GROUP, BUNDLE))


def next_residual(sc, res, val, bundles, out):
    at = 0
    for piece in partner_pieces(sc, *bundles, 1, 0):
        end = at + piece.shape[0]
        out[at:end, :] = res[at:end, :] - (val[at:end, :] + piece)
        at = end


def step_kernel(sc, res, val, bt, xa, xb, ya, yb, za, zb, res_ref, out):
    next_residual(sc, res, val, (xa, xb, ya, yb, za, zb), res_ref)
    project(sc, bt, res_ref[...], out)


def last_kernel(sc, res, val, inv, xa, xb, ya, yb, za, zb, out, scratch):
    next_residual(sc, res, val, (xa, xb, ya, yb, za, zb), scratch)
    out[...] = dot_wide(inv[...], scratch[...])


def unpack_kernel(sc, inv, val, out):
    out[...] = dot_wide(inv[...], val[...])


def mode_kernel(sc, cols, comp, block, out):
    pick = jnp.where(iota((ROWS, 128), 0) // GROUP == iota((ROWS, 128), 1), 1.0, 0.0).astype(BF16)
    wide = dot(pick, comp[...].astype(BF16))
    keep = iota((ROWS, 128), 0) % GROUP == iota((ROWS, 128), 1) // 16
    wide = jnp.where(keep, wide, 0.0).astype(BF16)
    mode = iota((128, STACK), 0) % 16
    fold = jnp.where(mode == iota((128, STACK), 1) % NMODE, 1.0, 0.0).astype(BF16)
    theirs = dot(wide, fold)
    mode = iota((16, STACK), 0)
    own = jnp.where(mode == iota((16, STACK), 1) % NMODE, 1.0, 0.0).astype(BF16)
    mine = dot(cols[...], own)
    x_even, y_even = sc[0] == 0, sc[1] == 0
    which = jnp.where(
        x_even,
        jnp.where(y_even, block[:, 0:1], block[:, 1:2]),
        jnp.where(y_even, block[:, 2:3], block[:, 3:4]),
    )
    which = which + sc[2]
    at = iota((ROWS, STACK), 1) // NMODE
    home = 16 * sc[0] + 4 * sc[1] + 1 + sc[2]
    out[...] = (jnp.where(at == which, theirs, 0.0) + jnp.where(at == home, mine, 0.0)).astype(BF16)


def line_kernel(sc, line, inverse, mat_ref, out):
    everyone = line[...]
    size, coarse = everyone.shape[0], inverse.shape[0]
    counts = jnp.where(iota((size, 128), 0) % 8 == NMODE, everyone, 0.0).astype(BF16)

    def selection(rows, unit, first):
        position = iota((rows, size), 0) // unit + first
        col = iota((rows, size), 1)
        is_count = col % 8 == NMODE
        here = jnp.where(is_count & (col // 8 == position), 1.0, 0.0)
        before = jnp.where(is_count & (col // 8 < position), 1.0, 0.0)
        count = dot(here.astype(BF16), counts)
        offset = dot(before.astype(BF16), counts)
        mode = (iota((rows, 128), 0) % unit).astype(F32)
        compact = iota((rows, 128), 1).astype(F32)
        hit = (compact == offset + mode) & (mode < count)
        return jnp.where(hit, 1.0, 0.0)[:, 0:coarse]

    everywhere = selection(size, 8, 0)
    near = selection(NEAR, NMODE, sc[3] - sc[2] - 1)
    rows = jnp.dot(near, inverse[...], precision=HIGHEST, preferred_element_type=F32)
    matrix = lax.dot_general(rows, everywhere, (((1,), (1,)), ((), ())), precision=HIGHEST, preferred_element_type=F32)
    mat_ref[...] = matrix
    out[...] = jnp.dot(matrix, everyone, precision=HIGHEST, preferred_element_type=F32)


def solve_kernel(sc, line, matrix, out):
    out[...] = jnp.dot(matrix[...], line[...], precision=HIGHEST, preferred_element_type=F32)


def advance_kernel(keep, take, sc, *refs):
    if keep:
        res, modes, dual_a, dual_b, stack, old_dir, old_mul, dir_ref, mul_ref, val_ref, sa, sb = refs
    else:
        res, modes, dual_a, dual_b, stack, dir_ref, val_ref, sa, sb = refs
    corrected = res[...] - dot_wide(modes[...], stack[...])
    if keep:
        direction = keep * old_dir[...] + take * corrected
        mul_ref[...] = old_mul[...] + direction
    else:
        direction = corrected / take
    dir_ref[...] = direction
    rounded = direction.astype(BF16)
    val_ref[0 : ROWS // 2, :] = dot(dual_a[...], rounded)
    val_ref[ROWS // 2 :, :] = dot(dual_b[...], rounded)
    send_x(sc[0], (val_ref,), sa, sb, False)


def share(block, axis):
    size, line = lax.axis_size(axis), lax.axis_size("gz")
    groups = []
    for z in range(line):
        for even in range(0, size, 2):
            odd = even + 1 if z % 2 == 0 else even - 1
            if odd >= 0:
                groups.append([even * line + z, odd * line + z])
            elif line % 4:
                groups.append([z, (size - 1) * line + z])
            elif z % 4 == 1:
                for end in (0, size - 1):
                    groups.append([end * line + z, end * line + z + 2])
    block = lax.all_gather(block, (axis, "gz"), axis_index_groups=groups, tiled=True)
    return lax.all_gather(block, "gz", axis_index_groups=[[z, z + 1] for z in range(0, line, 2)], tiled=True)


def label(sign, odd):
    if sign == 0:
        return odd
    if odd:
        return 2 if sign == 1 else 0
    return 1 if sign == 1 else 3


def amplitude_blocks():
    out = np.zeros((ROWS, 4), np.int32)
    for x_odd in (0, 1):
        for y_odd in (0, 1):
            for (o1, o2, o3), _, width in SLOTS:
                at = OURS[(o1, o2, o3)]
                block = 4 * (4 * label(o1, x_odd) + label(o2, y_odd)) + o3 + 1
                out[at : at + width, 2 * x_odd + y_odd] = block
    return out


def cross(sc, value, x):
    pair = [((BUNDLE, 128), F32)] * 2
    y = exchange(*call(functools.partial(route_y, False), pair, sc, value, *x, name="route_y"), "gy")
    z = exchange(*call(functools.partial(route_z, False), pair, sc, value, *x, *y, name="route_z"), "gz")
    return (*x, *y, *z)


def local(dual_blocks, load_terms, row_order, mode_rows, mode_count, coarse_inverse):
    line_length = lax.axis_size("gz")
    pos = [lax.axis_index(axis) for axis in ("gx", "gy", "gz")]
    sc = jnp.stack([p % 2 for p in pos] + [pos[2], mode_count[0, 0, 0]]).astype(jnp.int32)
    inverse = in_hbm(coarse_inverse[0, 0])
    bundle = [((BUNDLE, 128), F32)] * 2
    vector = ((ROWS, 128), F32)
    square = ((ROWS, ROWS), BF16)
    wide = [((bundle_rows(True), 128), F32)] * 2
    gathered = ((line_length, 8, 128), F32)

    sel, load_rows, comp, mode, cols, order, sa, sb = pl.pallas_call(
        pack_kernel,
        out_shape=[
            jax.ShapeDtypeStruct(*v)
            for v in (
                square,
                vector,
                ((ROWS // GROUP, 128), F32),
                ((16, ROWS), BF16),
                ((ROWS, 16), BF16),
                ((ROWS // 128, 128), jnp.int32),
                *wide,
            )
        ],
        in_specs=[SMEM, HBM, HBM, HBM],
        out_specs=[VMEM] * 8,
        scratch_shapes=[
            pltpu.VMEM((ROWS, 1), jnp.int32),
            pltpu.VMEM((ROWS, 128), BF16),
            pltpu.VMEM((NMODE, ROWS), BF16),
            pltpu.SemaphoreType.DMA((3,)),
        ],
        compiler_params=pltpu.CompilerParams(vmem_limit_bytes=16 * 2**20),
        name="pack",
    )(sc, in_hbm(row_order[0, 0, 0].reshape(ROWS // 128, 128)), in_hbm(load_terms[0, 0, 0]), in_hbm(mode_rows[0, 0, 0].T))
    half = ((ROWS // 2, ROWS), BF16)
    x = exchange_async(sa, sb, "gx")
    dual_a, inv, bt = pl.pallas_call(
        permute_kernel,
        out_shape=[jax.ShapeDtypeStruct(*v) for v in (half, square, ((16, ROWS), BF16))],
        in_specs=[VMEM, VMEM, VMEM, HBM],
        out_specs=[VMEM] * 3,
        scratch_shapes=[pltpu.VMEM((ROWS, ROWS), BF16), pltpu.SemaphoreType.DMA],
        compiler_params=pltpu.CompilerParams(vmem_limit_bytes=16 * 2**20),
        name="permute",
    )(sel, mode, order, in_hbm(dual_blocks[0, 0, 0]))
    *x, dual_a, inv, bt = lax.optimization_barrier((*x, dual_a, inv, bt))
    values = (load_rows, comp)
    y = exchange_async(*call(functools.partial(route_y, True), wide, sc, *values, *x, name="route_y"), "gy")
    dual_b, near_inverse = pl.pallas_call(
        functools.partial(permute_rest_kernel, ROWS // 2),
        out_shape=[jax.ShapeDtypeStruct(*half), jax.ShapeDtypeStruct(inverse.shape, F32)],
        in_specs=[VMEM] * 3 + [HBM],
        out_specs=[VMEM] * 2,
        scratch_shapes=[pltpu.SemaphoreType.DMA],
        compiler_params=pltpu.CompilerParams(vmem_limit_bytes=12 * 2**20),
        name="permute_rest",
    )(sel, inv, dual_blocks[0, 0, 0], inverse)
    *y, dual_b, near_inverse = lax.optimization_barrier((*y, dual_b, near_inverse))
    z = exchange(*call(functools.partial(route_z, True), wide, sc, *values, *x, *y, name="route_z"), "gz")
    received_rows = (*x, *y, *z)
    residual, their_comp, proj = call(
        first_kernel,
        [vector, ((ROWS // GROUP, 128), F32), gathered],
        sc,
        load_rows,
        bt,
        *received_rows,
        name="first",
    )
    center_value = 0.5 * (EIG_HIGH + EIG_LOW)
    half_width = 0.5 * (EIG_HIGH - EIG_LOW)
    rho_prev = half_width / center_value
    amp = ((NEAR, 128), F32)
    for iteration in range(ITERS):
        line = lax.all_to_all(proj, "gz", 0, 0, tiled=True).reshape(8 * line_length, 128)
        if iteration == 0:
            near_matrix = ((NEAR, 8 * line_length), F32)
            matrix, own = call(line_kernel, [near_matrix, amp], sc, line, near_inverse, name="line")
            their_comp, own = lax.optimization_barrier((their_comp, own))
            (modes_near,) = call(
                mode_kernel, [((ROWS, STACK), BF16)], sc, cols, their_comp, jnp.asarray(amplitude_blocks()), name="modes"
            )
        else:
            (own,) = call(solve_kernel, [amp], sc, line, matrix, name="solve")
        near = (modes_near, dual_a, dual_b, share(share(own, "gy"), "gx"))
        if iteration == 0:
            direction, value, sa, sb = call(
                functools.partial(advance_kernel, None, center_value),
                [vector, vector, *bundle],
                sc,
                residual,
                *near,
                name="advance0",
            )
            multipliers = direction
        else:
            rho_now = 1.0 / (2.0 * center_value / half_width - rho_prev)
            direction, multipliers, value, sa, sb = call(
                functools.partial(advance_kernel, rho_now * rho_prev, 2.0 * rho_now / half_width),
                [vector, vector, vector, *bundle],
                sc,
                residual,
                *near,
                direction,
                multipliers,
                name="advance",
            )
            rho_prev = rho_now
        if iteration < ITERS - 1:
            received_rows = cross(sc, value, exchange(sa, sb, "gx"))
            residual, proj = call(
                step_kernel, [vector, gathered], sc, residual, value, bt, *received_rows, name="step"
            )
    x = exchange_async(sa, sb, "gx")
    (out_mul,) = call(unpack_kernel, [vector], sc, inv, multipliers, name="unpack")
    *x, out_mul = lax.optimization_barrier((*x, out_mul))
    received_rows = cross(sc, value, x)
    (out_res,) = call(
        last_kernel,
        [vector],
        sc,
        residual,
        value,
        inv,
        *received_rows,
        scratch=[pltpu.VMEM((ROWS, 128), F32)],
        name="last",
    )
    return out_mul[None, None, None], out_res[None, None, None]


def solution(mesh):
    in_specs = (
        P("gx", "gy", "gz", None, None),
        P("gx", "gy", "gz", None, None),
        P("gx", "gy", "gz", None),
        P("gx", "gy", "gz", None, None),
        P("gx", "gy", "gz"),
        P("gx", "gy", None, None),
    )
    out_specs = (P("gx", "gy", "gz", None, None), P("gx", "gy", "gz", None, None))
    return jax.shard_map(local, mesh=mesh, in_specs=in_specs, out_specs=out_specs, check_vma=False)
```
